256 devices in a mesh: batch: 32 (over z_lo, y, core), seq: 8 (over z_hi, x).
Axes of the slice: x: 4, y: 4, z: 8 (z_hi: 2, z_lo: 4; z = z_hi * 4 + z_lo), core: 2. Of those that a mesh axis runs over, the one named last changes fastest.
Arguments:
- tokens: bfloat16 [32, 1024, 1536], P('batch', 'seq'), may hold values from -13.3 to 13.3
- w_conv: bfloat16 [1536, 3, 384], replicated, may hold values from -0.09375 to 0.09375
- w_point: bfloat16 [1536, 384], replicated, may hold values from -0.3125 to 0.3125
- exon_table: int32 [32, 3, 256], P('batch'), may hold values from 0 to 1024, as said below
- gene_grads: bfloat16 [32, 64, 1536], P('batch', 'seq'), may hold values from -6 to 6
Outputs:
- pooled: float32 [32, 64, 1536], P('batch', 'seq')
- grad_input: bfloat16 [32, 1024, 1536], P('batch', 'seq')
- grad_conv: float32 [1536, 3, 384], P(('batch', 'seq'))
The draws below stay inside these ranges and needn't reach their ends.
Inputs may be any that keep to these rules, and one draw needn't show every extreme that they name: exon_table[w, 0, e] is exon e's gene, 0 to 63; exon_table[w, 1, e] its first bin and exon_table[w, 2, e] one past its last bin; every exon covers 1 to 32 bins and some exon of each window exactly 32; exons may intersect and a gene may have any number of exons.
All inputs are finite; a program needn't handle non-finite values.
Results may differ from the reference program's by a relative error of at most 0.008.
Values may be sent and summed in bfloat16 or wider, within the bound.
No kernel may reach another device: no remote copies, remote signals or barrier semaphores. Data moves between devices by JAX's collectives and lax.ppermute only.
A program may use at most 128 MiB of HBM per device.

```python
import jax
import jax.numpy as jnp
from jax import lax

C = 1536
HID = 384
DILATION = 4
GENES = 64
EXONS = 256
EXON_LEN = 32
WINDOWS = 32
BINS = 1024


def draw_tokens(key, part):
    first_key, second_key, third_key = jax.random.split(key, 3)
    array_shape = (WINDOWS, BINS, C)
    base_values = jnp.clip(jax.random.normal(first_key, array_shape, jnp.float32), -4.0, 4.0)
    column_scale = jnp.exp(jax.random.uniform(second_key, (C,), jnp.float32, -0.6, 0.6))
    row_scale = jnp.exp(jax.random.uniform(third_key, (WINDOWS, BINS, 1), jnp.float32, -0.6, 0.6))
    return (base_values * column_scale * row_scale).astype(jnp.bfloat16)


def draw_exon_table(key, part):
    first_key, second_key, third_key = jax.random.split(key, 3)
    gene_ids = jax.random.randint(first_key, (WINDOWS, EXONS), 0, GENES)
    lengths = jax.random.randint(second_key, (WINDOWS, EXONS), 1, EXON_LEN + 1)
    lengths = lengths.at[:, 0].set(EXON_LEN)
    starts = jax.random.randint(third_key, (WINDOWS, EXONS), 0, BINS - lengths + 1)
    starts = starts.at[:, 0].set(0)
    starts = starts.at[:, 1].set(BINS - lengths[:, 1])
    exon_ends = starts + lengths
    return jnp.stack([gene_ids, starts, exon_ends], axis=1).astype(jnp.int32)


def block_scale(own_key, extent, shards, low, high):
    level, own = 1.0, jax.random.fold_in(own_key, 6)
    for position, parts in shards:
        heights = jnp.exp(jax.random.uniform(jax.random.fold_in(own, position), (parts,), jnp.float32, low / len(shards), high / len(shards)))
        level = level * jnp.repeat(heights, extent[position] // parts).reshape([-1 if axis == position else 1 for axis in range(len(extent))])
    return level


def gaussian(own_key, shape, scale, bound, pieces=(), kind=jnp.bfloat16):
    values = jax.random.normal(own_key, shape, jnp.float32) * scale
    if len(pieces) > 0:
        values = block_scale(own_key, shape, pieces, -0.22, 0.18) * values
    return jnp.clip(values, min=-bound, max=bound).astype(kind)


def setup_inputs(seed: int = 0) -> dict:
    key_of = jax.random.split(jax.random.key(seed), 6)
    return {
        "tokens": draw_tokens(jax.random.fold_in(key_of[5], 71), 0),
        "w_conv": gaussian(key_of[1], (C, 3, HID), (3 * C) ** -0.5, 0.09375),
        "w_point": gaussian(key_of[2], (C, HID), HID ** -0.5, 0.3125),
        "exon_table": draw_exon_table(jax.random.fold_in(key_of[5], 71), 0),
        "gene_grads": gaussian(key_of[4], (WINDOWS, GENES, C), 1.0, 6.0, ((0, 32), (1, 8))),
    }


EPSILON = 1e-06
INVERSE_ROOT_TWO = 0.7071067811865476
INVERSE_ROOT_TAU = 0.3989422804014327

def cumulative(values):
    return 0.5 * (1.0 + lax.erf(values * INVERSE_ROOT_TWO))

def gelu_value(values):
    return values * cumulative(values)

def gelu_slope(values):
    return cumulative(values) + values * jnp.exp(-0.5 * values * values) * INVERSE_ROOT_TAU

def reverse_both(values):
    return values[::-1, ::-1]

def pool_matrix(table, first_bin, bin_count):
    gene_ids = table[0]
    starts = table[1]
    exon_ends = table[2]
    positions = first_bin + jnp.arange(bin_count, dtype=jnp.int32)
    inside = ((positions[None, :] >= starts[:, None]) & (positions[None, :] < exon_ends[:, None])).astype(jnp.bfloat16)
    member = (gene_ids[:, None] == jnp.arange(GENES, dtype=jnp.int32)[None, :]).astype(jnp.bfloat16)
    counts = lax.dot_general(member, inside, (((0,), (0,)), ((), ())), preferred_element_type=jnp.float32)
    return counts.astype(jnp.bfloat16)

def conv_forward(normed_in, flat_conv):
    span = normed_in.shape[0]
    hidden_units = flat_conv.shape[1] // 3
    padded = jnp.pad(normed_in, ((DILATION, DILATION), (0, 0)))
    products = jnp.dot(padded, flat_conv, preferred_element_type=jnp.float32)
    total = products[0:span, 0:hidden_units]
    total = total + products[DILATION:DILATION + span, hidden_units:2 * hidden_units]
    return total + products[2 * DILATION:2 * DILATION + span, 2 * hidden_units:]

def conv_backward(grad_pre, flat_conv):
    span = grad_pre.shape[0]
    padded = jnp.pad(grad_pre, ((DILATION, DILATION), (0, 0)))
    stacked = jnp.concatenate([padded[2 * DILATION:2 * DILATION + span], padded[DILATION:DILATION + span], padded[0:span]], axis=1)
    return lax.dot_general(stacked, flat_conv, (((1,), (1,)), ((), ())), preferred_element_type=jnp.float32)

def weight_terms(normed_in, grad_pre):
    span = normed_in.shape[0]
    padded = jnp.pad(normed_in, ((DILATION, DILATION), (0, 0)))
    tap_list = []
    for tap_number in range(3):
        shifted = padded[tap_number * DILATION:tap_number * DILATION + span]
        tap_list.append(lax.dot_general(shifted, grad_pre, (((0,), (0,)), ((), ())), preferred_element_type=jnp.float32))
    return jnp.stack(tap_list, axis=1)

def window_pass(tokens, w_conv, w_point, table, grads):
    span, channels = tokens.shape
    hidden_units = w_conv.shape[2]
    flat_conv = w_conv.reshape(channels, 3 * hidden_units)
    wide = tokens.astype(jnp.float32)
    scale = lax.rsqrt(lax.optimization_barrier(jnp.mean(wide * wide, axis=1, keepdims=True)) + EPSILON)
    unit = wide * scale
    normed = unit.astype(jnp.bfloat16)
    inputs = [normed, reverse_both(normed)]
    preacts = [conv_forward(branch_in, flat_conv) for branch_in in inputs]
    activations = [gelu_value(preact).astype(jnp.bfloat16) for preact in preacts]
    outputs = []
    for activation in activations:
        projected = lax.dot_general(activation, w_point, (((1,), (1,)), ((), ())), preferred_element_type=jnp.float32)
        outputs.append(lax.optimization_barrier(projected.astype(jnp.bfloat16)))
    block = (wide + outputs[0].astype(jnp.float32) + reverse_both(outputs[1]).astype(jnp.float32)).astype(jnp.bfloat16)
    pool = pool_matrix(table, 0, span)
    pooled = jnp.dot(pool, block, preferred_element_type=jnp.float32)
    bin_grad = lax.dot_general(pool, grads, (((0,), (0,)), ((), ())), preferred_element_type=jnp.float32).astype(jnp.bfloat16)
    out_grads = [bin_grad, reverse_both(bin_grad)]
    units = [unit, reverse_both(unit)]
    scales = [scale, scale[::-1]]
    token_grads = []
    terms = jnp.zeros((channels, 3, hidden_units), jnp.float32)
    for branch_number in range(2):
        grad_act = jnp.dot(out_grads[branch_number], w_point, preferred_element_type=jnp.float32)
        grad_pre = (grad_act * gelu_slope(preacts[branch_number])).astype(jnp.bfloat16)
        grad_normed = conv_backward(grad_pre, flat_conv)
        unit_part = units[branch_number]
        centred = grad_normed - unit_part * lax.optimization_barrier(jnp.mean(grad_normed * unit_part, axis=1, keepdims=True))
        token_grads.append(lax.optimization_barrier((centred * scales[branch_number]).astype(jnp.bfloat16)))
        terms = terms + weight_terms(inputs[branch_number], grad_pre)
    kept_grad = lax.optimization_barrier(bin_grad)
    grad_input = (kept_grad.astype(jnp.float32) + token_grads[0].astype(jnp.float32) + reverse_both(token_grads[1]).astype(jnp.float32)).astype(jnp.bfloat16)
    return (pooled, grad_input, terms)

def reference(tokens, w_conv, w_point, exon_table, gene_grads):

    def one_window(carry, window):
        window_tokens, table, grads = window
        pooled, grad_input, terms = window_pass(window_tokens, w_conv, w_point, table, grads)
        return (carry + terms, (pooled, grad_input))
    initial = jnp.zeros((C, 3, HID), jnp.float32)
    total, (pooled, grad_input) = lax.scan(one_window, initial, (tokens, exon_table, gene_grads))
    total = total * (1.0 / WINDOWS)
    return (pooled, grad_input, total)
```

```python
import jax
import jax.numpy as jnp
import numpy as np
from jax import lax
from jax.experimental import pallas as pl
from jax.experimental.pallas import tpu as pltpu
from jax.sharding import PartitionSpec as P

DILATION = 4
GENES = 64
EPSILON = 1e-06
INVERSE_ROOT_TWO = 0.7071067811865476
INVERSE_ROOT_TAU = 0.3989422804014327

BINS = 128
HALO = 8
ROWS = BINS + 2 * HALO
C = 1536
HID = 384
HALF = C // 2
FLIP = 256
BF = jnp.bfloat16
F32 = jnp.float32
VMEM_LIMIT = 48 * 1024 * 1024

CORE_PAIRS = [(b, b ^ 1) for b in range(32)]


def linear(z_hi, x, z_lo, y, core):
    return ((z_lo * 4 + y) * 2 + core) * 8 + z_hi * 4 + x


PLANES = [
    [linear(zh, x, zl, y, c) for y in range(4) for x in range(4)]
    for zh in range(2)
    for zl in range(4)
    for c in range(2)
]
COLUMNS = [
    [linear(zh, x, zl, y, c) for zh in range(2) for zl in range(4)]
    for x in range(4)
    for y in range(4)
    for c in range(2)
]
CHANNELS = np.array(
    [
        6 * linear(zh, x, zl, y, 0) + k
        for y in range(4)
        for x in range(4)
        for zh in range(2)
        for zl in range(4)
        for k in range(6)
    ],
    dtype=np.int32,
).reshape(HALF, 1)


def dot(a, b, da, db):
    return lax.dot_general(a, b, (((da,), (db,)), ((), ())), preferred_element_type=F32)


def cumulative(values):
    return 0.5 * (1.0 + lax.erf(values * INVERSE_ROOT_TWO))


def gelu_value(values):
    return values * cumulative(values)


def gelu_slope(values):
    return cumulative(values) + values * jnp.exp(-0.5 * values * values) * INVERSE_ROOT_TAU


def reverser():
    rows = lax.broadcasted_iota(jnp.int32, (FLIP, FLIP), 0)
    cols = lax.broadcasted_iota(jnp.int32, (FLIP, FLIP), 1)
    return jnp.where(rows + cols == FLIP - 1, 1.0, 0.0).astype(BF)


def flip_channels(values, turn):
    parts = []
    for k in reversed(range(C // FLIP)):
        parts.append(dot(values[:, k * FLIP : (k + 1) * FLIP], turn, 1, 0).astype(BF))
    return jnp.concatenate(parts, axis=1)


def row_scale(wide):
    return lax.rsqrt(jnp.mean(wide * wide, axis=1, keepdims=True) + EPSILON)


def pool_inside(table, first_bin, rows):
    positions = first_bin + lax.broadcasted_iota(jnp.int32, (rows, table.shape[1]), 0)
    inside = (positions >= table[1:2, :]) & (positions < table[2:3, :])
    return jnp.where(inside, 1.0, 0.0).astype(BF)


def pool_member(table):
    genes = lax.broadcasted_iota(jnp.int32, (GENES, table.shape[1]), 0)
    return jnp.where(genes == table[0:1, :], 1.0, 0.0).astype(BF)


def forward_kernel(left, tok, right, wc, pre):
    wide = jnp.concatenate([left[...].astype(F32), tok[...].astype(F32), right[...].astype(F32)], axis=0)
    normed = (wide * row_scale(wide)).astype(BF)
    both = jnp.concatenate([normed, flip_channels(normed, reverser())], axis=0)
    rows = BINS + 2 * DILATION
    main = jnp.zeros((rows, HID), F32)
    mirror = jnp.zeros((rows, HID), F32)
    for tap in range(3):
        product = dot(both, wc[tap], 1, 0)
        main = main + product[tap * DILATION : tap * DILATION + rows]
        at = ROWS + (2 - tap) * DILATION
        mirror = mirror + product[at : at + rows]
    pre[0, 0:rows] = main
    pre[1, 0:rows] = mirror
    pre[:, rows:ROWS] = jnp.zeros((2, ROWS - rows, HID), F32)


def slope_kernel(first, pre, wp, grads, table, gp, bin_grad):
    inside = pool_inside(table[...], first[0] - DILATION, ROWS)
    counts = dot(inside, pool_member(table[...]), 1, 1).astype(BF)
    wide = dot(counts, grads[...], 1, 0)
    covered = wide.astype(BF)
    bin_grad[...] = wide[DILATION : DILATION + BINS].astype(BF)
    both = jnp.concatenate([covered, flip_channels(covered, reverser())], axis=0)
    grad_act = dot(both, wp[...], 1, 0)
    gp[0] = (grad_act[0:ROWS] * gelu_slope(pre[0])).astype(BF)
    gp[1] = (grad_act[ROWS:] * gelu_slope(pre[1])).astype(BF)


def turn_kernel(core, own, other, channels, out):
    wide = jnp.concatenate([own[...].astype(F32), other[...].astype(F32)], axis=0)
    normed = (wide * row_scale(wide)).astype(BF)
    wanted = channels[...] + 48 * core[0]
    main = jnp.zeros((HALF, 2 * BINS), F32)
    mirror = jnp.zeros((HALF, 2 * BINS), F32)
    for k in range(C // FLIP):
        lane = k * FLIP + lax.broadcasted_iota(jnp.int32, (HALF, FLIP), 1)
        piece = normed[:, k * FLIP : (k + 1) * FLIP]
        pick = jnp.where(lane == wanted, 1.0, 0.0).astype(BF)
        main = main + dot(pick, piece, 1, 1)
        pick = jnp.where(C - 1 - lane == wanted, 1.0, 0.0).astype(BF)
        mirror = mirror + dot(pick, piece, 1, 1)
    out[:, 0 : 2 * BINS] = main.astype(BF)
    out[:, 2 * BINS :] = mirror.astype(BF)


def weight_kernel(turned, own, other, out):
    wide = [[ref[branch].astype(F32) for ref in (own, other)] for branch in range(2)]
    for tap in range(3):
        parts = []
        for branch in range(2):
            at = (2 - tap) * DILATION if branch == 0 else tap * DILATION
            for window in range(2):
                parts.append(wide[branch][window][at : at + BINS].astype(BF))
        total = dot(turned[...], jnp.concatenate(parts, axis=0), 1, 0) * (1.0 / 32)
        out[:, tap] = total.astype(BF).reshape(16, 48, HID)


def output_kernel(first, tok, pre, wp, table, partial):
    table_rows = table[...]
    acts = [gelu_value(pre[branch, DILATION : DILATION + BINS]).astype(BF) for branch in range(2)]
    outs = dot(jnp.concatenate(acts, axis=0), wp[...], 1, 1).astype(BF)
    mirror = flip_channels(outs[BINS:], reverser())
    block = (tok[...].astype(F32) + outs[0:BINS].astype(F32) + mirror.astype(F32)).astype(BF)
    inside = pool_inside(table_rows, first[0], BINS)
    counts = dot(pool_member(table_rows), inside, 1, 1).astype(BF)
    partial[...] = dot(counts, block, 1, 0).astype(BF)


def input_kernel(tok, gp, bin_grad, wc, out):
    wide = tok[...].astype(F32)
    scale = row_scale(wide)
    unit = wide * scale
    turn = reverser()
    mirror_unit = flip_channels(tok[...], turn).astype(F32) * scale
    shifted = [gp[0].astype(F32), gp[1].astype(F32)]
    total = jnp.zeros((2 * BINS, C), F32)
    for tap in range(3):
        main = shifted[0][(2 - tap) * DILATION : (2 - tap) * DILATION + BINS]
        mirror = shifted[1][tap * DILATION : tap * DILATION + BINS]
        total = total + dot(jnp.concatenate([main, mirror], axis=0).astype(BF), wc[tap], 1, 1)
    parts = []
    for grad, part in ((total[0:BINS], unit), (total[BINS:], mirror_unit)):
        centred = grad - part * jnp.mean(grad * part, axis=1, keepdims=True)
        parts.append((centred * scale).astype(BF))
    mirror = flip_channels(parts[1], turn)
    out[...] = (bin_grad[...].astype(F32) + parts[0].astype(F32) + mirror.astype(F32)).astype(BF)


def call(kernel, out_shape, *args, scalars=0):
    specs = [pl.BlockSpec(memory_space=pltpu.SMEM)] * scalars
    specs += [pl.BlockSpec(memory_space=pltpu.VMEM)] * (len(args) - scalars)
    return pl.pallas_call(
        kernel,
        out_shape=out_shape,
        in_specs=specs,
        compiler_params=pltpu.CompilerParams(vmem_limit_bytes=VMEM_LIMIT),
    )(*args)


def shape(dims, kind):
    return jax.ShapeDtypeStruct(dims, kind)


def scatter_genes(partial, position):
    values = partial.astype(F32)
    for bit in (1, 0, 2):
        mine = (position >> bit) & 1
        rows = values.reshape(-1, 2, ROWS_AFTER[bit], C)
        keep = jnp.where(mine == 0, rows[:, 0], rows[:, 1])
        give = jnp.where(mine == 0, rows[:, 1], rows[:, 0]).astype(BF)
        got = lax.ppermute(give, "seq", [(s, s ^ (1 << bit)) for s in range(8)])
        values = (keep + got.astype(F32)).reshape(-1, C)
    return values


ROWS_AFTER = {1: 16, 0: 8, 2: 8}


def local(tokens, w_conv, w_point, exon_table, gene_grads):
    tok = tokens[0]
    table = exon_table[0]
    position = lax.axis_index("seq")
    core = (lax.axis_index("batch") & 1).astype(jnp.int32).reshape(1)
    first = (position * BINS).astype(jnp.int32).reshape(1)
    taps = jnp.transpose(w_conv, (1, 0, 2))

    left = lax.ppermute(tok[BINS - HALO :], "seq", [(s, s + 1) for s in range(7)])
    right = lax.ppermute(tok[:HALO], "seq", [(s + 1, s) for s in range(7)])
    other = lax.ppermute(tok, "batch", CORE_PAIRS)
    spread = jnp.broadcast_to(gene_grads, (8,) + gene_grads.shape[1:])
    grads = lax.all_to_all(spread, "seq", 0, 0, tiled=True).reshape(GENES, C)

    pre = call(forward_kernel, shape((2, ROWS, HID), F32), left, tok, right, taps)
    turned = call(
        turn_kernel, shape((HALF, 4 * BINS), BF), core, tok, other, jnp.asarray(CHANNELS), scalars=1
    )
    gp, bin_grad = call(
        slope_kernel,
        (shape((2, ROWS, HID), BF), shape((BINS, C), BF)),
        first,
        pre,
        w_point,
        grads,
        table,
        scalars=1,
    )
    gp_other = lax.ppermute(gp, "batch", CORE_PAIRS)
    terms = call(weight_kernel, shape((16, 3, 48, HID), BF), turned, gp, gp_other)
    terms = lax.all_to_all(terms, ("batch", "seq"), 0, 0, tiled=True, axis_index_groups=PLANES)
    terms = jnp.sum(terms.astype(F32), axis=0).astype(BF)
    terms = jnp.transpose(terms.reshape(3, 8, 6, HID), (1, 2, 0, 3))
    terms = lax.all_to_all(terms, ("batch", "seq"), 0, 0, tiled=True, axis_index_groups=COLUMNS)
    total = jnp.sum(terms.astype(F32), axis=0)

    partial = call(
        output_kernel, shape((GENES, C), BF), first, tok, pre, w_point, table, scalars=1
    )
    pooled = scatter_genes(partial, position)
    grad_input = call(input_kernel, shape((BINS, C), BF), tok, gp, bin_grad, taps)
    return (pooled[None], grad_input[None], total)


def solution(mesh):
    placed = (P("batch", "seq", None), P(), P(), P("batch", None, None), P("batch", "seq", None))
    return jax.shard_map(
        local,
        mesh=mesh,
        in_specs=placed,
        out_specs=(
            P("batch", "seq", None),
            P("batch", "seq", None),
            P(("batch", "seq"), None, None),
        ),
        check_vma=False,
    )
```

```python
import jax
import jax.numpy as jnp
import numpy as np
from jax import lax
from jax.experimental import pallas as pl
from jax.experimental.pallas import tpu as pltpu
from jax.sharding import PartitionSpec as P

DILATION = 4
GENES = 64
EPSILON = 1e-06
INVERSE_ROOT_TWO = 0.7071067811865476
INVERSE_ROOT_TAU = 0.3989422804014327

BINS = 128
PAIR = 2 * BINS
HALO = 8
ROWS = PAIR + 2 * HALO
C = 1536
HID = 384
QUARTER = C // 4
FLIP = 256
BF = jnp.bfloat16
F32 = jnp.float32
VMEM_LIMIT = 48 * 1024 * 1024

CORE_PAIRS = [(b, b ^ 1) for b in range(32)]
SEQ_PAIRS = [(s, s ^ 1) for s in range(8)]


def linear(z_hi, x, z_lo, y, core):
    return ((z_lo * 4 + y) * 2 + core) * 8 + z_hi * 4 + x


PLANES = [
    [linear(zh, 2 * half + odd, zl, y, c) for y in range(4) for half in range(2)]
    for odd in range(2)
    for zh in range(2)
    for zl in range(4)
    for c in range(2)
]
COLUMNS = [
    [linear(zh, x, zl, y, c) for zh in range(2) for zl in range(4)]
    for x in range(4)
    for y in range(4)
    for c in range(2)
]
CHANNELS = np.array(
    [
        6 * linear(zh, 2 * half, zl, y, 0) + k
        for y in range(4)
        for half in range(2)
        for zh in range(2)
        for zl in range(4)
        for k in range(6)
    ],
    dtype=np.int32,
).reshape(QUARTER, 1)


def dot(a, b, da, db):
    return lax.dot_general(a, b, (((da,), (db,)), ((), ())), preferred_element_type=F32)


def cumulative(values):
    return 0.5 * (1.0 + lax.erf(values * INVERSE_ROOT_TWO))


def gelu_value(values):
    return values * cumulative(values)


def gelu_slope(values):
    return cumulative(values) + values * jnp.exp(-0.5 * values * values) * INVERSE_ROOT_TAU


def reverser():
    rows = lax.broadcasted_iota(jnp.int32, (FLIP, FLIP), 0)
    cols = lax.broadcasted_iota(jnp.int32, (FLIP, FLIP), 1)
    return jnp.where(rows + cols == FLIP - 1, 1.0, 0.0).astype(BF)


def flip_channels(values, turn):
    parts = []
    for k in reversed(range(C // FLIP)):
        parts.append(dot(values[:, k * FLIP : (k + 1) * FLIP], turn, 1, 0).astype(BF))
    return jnp.concatenate(parts, axis=1)


def row_scale(wide):
    return lax.rsqrt(jnp.mean(wide * wide, axis=1, keepdims=True) + EPSILON)


def pool_inside(table, first_bin, rows):
    positions = first_bin + lax.broadcasted_iota(jnp.int32, (rows, table.shape[1]), 0)
    inside = (positions >= table[1:2, :]) & (positions < table[2:3, :])
    return jnp.where(inside, 1.0, 0.0).astype(BF)


def pool_member(table, genes):
    return jnp.where(genes == table[0:1, :], 1.0, 0.0).astype(BF)


def pack_kernel(position, tok, grads, out):
    odd = position[0] % 2
    head = tok[0:HALO].astype(F32)
    tail = tok[BINS - HALO : BINS].astype(F32)
    rows = jnp.concatenate([grads[...].astype(F32), jnp.where(odd == 1, tail, head)], axis=0).astype(BF)
    for seat in range(8):
        out[seat] = rows


def in_order(odd, own, partner):
    return jnp.where(odd == 0, own, partner), jnp.where(odd == 0, partner, own)


def forward_kernel(position, tok, partner, spread, wc, pre):
    pair = position[0] // 2
    left = spread[jnp.maximum(2 * pair - 1, 0)][8 : 8 + HALO].astype(F32)
    right = spread[jnp.minimum(2 * pair + 2, 7)][8 : 8 + HALO].astype(F32)
    left = jnp.where(pair > 0, left, 0.0)
    right = jnp.where(pair < 3, right, 0.0)
    low, high = in_order(position[0] % 2, tok[...].astype(F32), partner[...].astype(F32))
    wide = jnp.concatenate([left, low, high, right], axis=0)
    normed = (wide * row_scale(wide)).astype(BF)
    both = jnp.concatenate([normed, flip_channels(normed, reverser())], axis=0)
    rows = PAIR + 2 * DILATION
    main = jnp.zeros((rows, HID), F32)
    mirror = jnp.zeros((rows, HID), F32)
    for tap in range(3):
        product = dot(both, wc[tap], 1, 0)
        main = main + product[tap * DILATION : tap * DILATION + rows]
        at = ROWS + (2 - tap) * DILATION
        mirror = mirror + product[at : at + rows]
    pre[0, 0:rows] = main
    pre[1, 0:rows] = mirror
    pre[:, rows:ROWS] = jnp.zeros((2, ROWS - rows, HID), F32)


def slope_kernel(position, pre, wp, spread, table, gp, bin_grad, wide):
    first = (position[0] // 2) * PAIR - DILATION
    row = lax.broadcasted_iota(jnp.int32, (128, table.shape[1]), 0)
    genes = jnp.where((row & 15) < 8, (row >> 4) * 8 + (row & 7), -1)
    inside = pool_inside(table[...], first, ROWS)
    counts = dot(inside, pool_member(table[...], genes), 1, 1).astype(BF)
    wide[...] = dot(counts, spread[...].reshape(128, C), 1, 0)
    covered = wide[...].astype(BF)
    own = pl.multiple_of((position[0] % 2) * BINS, BINS)
    bin_grad[...] = wide[pl.ds(own, BINS + 8)][DILATION : DILATION + BINS].astype(BF)
    both = jnp.concatenate([covered, flip_channels(covered, reverser())], axis=0)
    grad_act = dot(both, wp[...], 1, 0)
    gp[0] = (grad_act[0:ROWS] * gelu_slope(pre[0])).astype(BF)
    gp[1] = (grad_act[ROWS:] * gelu_slope(pre[1])).astype(BF)


def turn_kernel(position, own, partner, other, other_partner, channels, out):
    odd = position[0] % 2
    blocks = in_order(odd, own[...], partner[...]) + in_order(odd, other[...], other_partner[...])
    normed = []
    for block in blocks:
        wide = block.astype(F32)
        normed.append((wide * row_scale(wide)).astype(BF))
    normed = jnp.concatenate(normed, axis=0)
    wanted = channels[...] + 6 * odd + 48 * position[1]
    main = jnp.zeros((QUARTER, 2 * PAIR), F32)
    mirror = jnp.zeros((QUARTER, 2 * PAIR), F32)
    for k in range(C // FLIP):
        lane = k * FLIP + lax.broadcasted_iota(jnp.int32, (QUARTER, FLIP), 1)
        piece = normed[:, k * FLIP : (k + 1) * FLIP]
        pick = jnp.where(lane == wanted, 1.0, 0.0).astype(BF)
        main = main + dot(pick, piece, 1, 1)
        pick = jnp.where(C - 1 - lane == wanted, 1.0, 0.0).astype(BF)
        mirror = mirror + dot(pick, piece, 1, 1)
    out[:, 0 : 2 * PAIR] = main.astype(BF)
    out[:, 2 * PAIR :] = mirror.astype(BF)


def weight_kernel(turned, own, other, out):
    wide = [[ref[branch].astype(F32) for ref in (own, other)] for branch in range(2)]
    for tap in range(3):
        parts = []
        for branch in range(2):
            at = (2 - tap) * DILATION if branch == 0 else tap * DILATION
            for window in range(2):
                parts.append(wide[branch][window][at : at + PAIR].astype(BF))
        total = dot(turned[...], jnp.concatenate(parts, axis=0), 1, 0) * (1.0 / 32)
        out[:, tap] = total.astype(BF).reshape(8, 48, HID)


def plane_sum_kernel(terms, out):
    total = terms[0].astype(F32)
    for k in range(1, 8):
        total = total + terms[k].astype(F32)
    for k in range(8):
        out[k] = total[:, 6 * k : 6 * k + 6].astype(BF)


def column_sum_kernel(terms, out):
    total = terms[0].astype(F32)
    for k in range(1, 8):
        total = total + terms[k].astype(F32)
    for tap in range(3):
        out[:, tap] = total[tap]


def own_rows(ref, branch, odd, before, after):
    start = pl.multiple_of(odd * BINS, BINS)
    return ref[branch, pl.ds(start, BINS + after)][before : before + BINS]


def output_kernel(position, tok, pre, wp, table, partial):
    odd = position[0] % 2
    acts = [gelu_value(own_rows(pre, branch, odd, DILATION, 8)).astype(BF) for branch in range(2)]
    outs = dot(jnp.concatenate(acts, axis=0), wp[...], 1, 1).astype(BF)
    mirror = flip_channels(outs[BINS:], reverser())
    block = (tok[...].astype(F32) + outs[0:BINS].astype(F32) + mirror.astype(F32)).astype(BF)
    genes = lax.broadcasted_iota(jnp.int32, (GENES, table.shape[1]), 0)
    inside = pool_inside(table[...], position[0] * BINS, BINS)
    counts = dot(pool_member(table[...], genes), inside, 1, 1).astype(BF)
    partial[...] = dot(counts, block, 1, 0)


def input_kernel(position, tok, gp, bin_grad, wc, out):
    odd = position[0] % 2
    wide = tok[...].astype(F32)
    scale = row_scale(wide)
    unit = wide * scale
    turn = reverser()
    mirror_unit = flip_channels(tok[...], turn).astype(F32) * scale
    start = pl.multiple_of(odd * BINS, BINS)
    shifted = [gp[branch, pl.ds(start, BINS + 16)].astype(F32) for branch in range(2)]
    total = jnp.zeros((2 * BINS, C), F32)
    for tap in range(3):
        main = shifted[0][(2 - tap) * DILATION : (2 - tap) * DILATION + BINS]
        mirror = shifted[1][tap * DILATION : tap * DILATION + BINS]
        total = total + dot(jnp.concatenate([main, mirror], axis=0).astype(BF), wc[tap], 1, 1)
    parts = []
    for grad, part in ((total[0:BINS], unit), (total[BINS:], mirror_unit)):
        centred = grad - part * jnp.mean(grad * part, axis=1, keepdims=True)
        parts.append((centred * scale).astype(BF))
    mirror = flip_channels(parts[1], turn)
    out[...] = (bin_grad[...].astype(F32) + parts[0].astype(F32) + mirror.astype(F32)).astype(BF)


def call(kernel, out_shape, *args, scalars=0, scratch=()):
    specs = [pl.BlockSpec(memory_space=pltpu.SMEM)] * scalars
    specs += [pl.BlockSpec(memory_space=pltpu.VMEM)] * (len(args) - scalars)
    return pl.pallas_call(
        kernel,
        out_shape=out_shape,
        in_specs=specs,
        scratch_shapes=scratch,
        compiler_params=pltpu.CompilerParams(vmem_limit_bytes=VMEM_LIMIT),
    )(*args)


def shape(dims, kind):
    return jax.ShapeDtypeStruct(dims, kind)


def scatter_genes(partial, position):
    values = partial
    for bit in (2, 1, 0):
        mine = (position >> bit) & 1
        half = values.shape[0] // 2
        keep = jnp.where(mine == 0, values[:half], values[half:])
        give = jnp.where(mine == 0, values[half:], values[:half]).astype(BF)
        got = lax.ppermute(give, "seq", [(s, s ^ (1 << bit)) for s in range(8)])
        values = keep + got.astype(F32)
    return values


def local(tokens, w_conv, w_point, exon_table, gene_grads):
    tok = tokens[0]
    table = exon_table[0]
    seat = lax.axis_index("seq").astype(jnp.int32)
    core = (lax.axis_index("batch") & 1).astype(jnp.int32)
    position = jnp.stack([seat, core])
    taps = jnp.transpose(w_conv, (1, 0, 2))

    spread = call(pack_kernel, shape((8, 16, C), BF), position, tok, gene_grads[0], scalars=1)
    spread = lax.all_to_all(spread, "seq", 0, 0, tiled=True)
    partner = lax.ppermute(tok, "seq", SEQ_PAIRS)
    other = lax.ppermute(tok, "batch", CORE_PAIRS)
    other_partner = lax.ppermute(partner, "batch", CORE_PAIRS)

    pre = call(
        forward_kernel, shape((2, ROWS, HID), F32), position, tok, partner, spread, taps, scalars=1
    )
    gp, bin_grad = call(
        slope_kernel,
        (shape((2, ROWS, HID), BF), shape((BINS, C), BF)),
        position,
        pre,
        w_point,
        spread,
        table,
        scalars=1,
        scratch=[pltpu.VMEM((ROWS, C), F32)],
    )
    gp_other = lax.ppermute(gp, "batch", CORE_PAIRS)
    turned = call(
        turn_kernel,
        shape((QUARTER, 4 * PAIR), BF),
        position,
        tok,
        partner,
        other,
        other_partner,
        jnp.asarray(CHANNELS),
        scalars=1,
    )
    terms = call(weight_kernel, shape((8, 3, 48, HID), BF), turned, gp, gp_other)
    terms = lax.all_to_all(terms, ("batch", "seq"), 0, 0, tiled=True, axis_index_groups=PLANES)
    terms = call(plane_sum_kernel, shape((8, 3, 6, HID), BF), terms)
    terms = lax.all_to_all(terms, ("batch", "seq"), 0, 0, tiled=True, axis_index_groups=COLUMNS)
    total = call(column_sum_kernel, shape((6, 3, HID), F32), terms)

    partial = call(
        output_kernel, shape((GENES, C), F32), position, tok, pre, w_point, table, scalars=1
    )
    pooled = scatter_genes(partial, seat)
    grad_input = call(
        input_kernel, shape((BINS, C), BF), position, tok, gp, bin_grad, taps, scalars=1
    )
    return (pooled[None], grad_input[None], total)


def solution(mesh):
    placed = (P("batch", "seq", None), P(), P(), P("batch", None, None), P("batch", "seq", None))
    return jax.shard_map(
        local,
        mesh=mesh,
        in_specs=placed,
        out_specs=(
            P("batch", "seq", None),
            P("batch", "seq", None),
            P(("batch", "seq"), None, None),
        ),
        check_vma=False,
    )
```

```python
import jax
import jax.numpy as jnp
import numpy as np
from jax import lax
from jax.experimental import pallas as pl
from jax.experimental.pallas import tpu as pltpu
from jax.sharding import PartitionSpec as P

DILATION = 4
GENES = 64
EPSILON = 1e-06
INVERSE_ROOT_TWO = 0.7071067811865476
INVERSE_ROOT_TAU = 0.3989422804014327

BINS = 128
PAIR = 2 * BINS
HALO = 8
ROWS = PAIR + 2 * HALO
C = 1536
HID = 384
QUARTER = C // 4
FLIP = 256
BF = jnp.bfloat16
F32 = jnp.float32
VMEM_LIMIT = 28 * 1024 * 1024

FORWARD_WORK = 2
TURN_WORK = 2
SLOPE_WORK = 2
OUTPUT_WORK = 0.3
INPUT_WORK = 1
SUM_WORK = 1
CORE_PAIRS = [(b, b ^ 1) for b in range(32)]
SEQ_PAIRS = [(s, s ^ 1) for s in range(8)]


def linear(z_hi, x, z_lo, y, core):
    return ((z_lo * 4 + y) * 2 + core) * 8 + z_hi * 4 + x


PLANES = [
    [linear(zh, 2 * half + odd, zl, y, c) for y in range(4) for half in range(2)]
    for odd in range(2)
    for zh in range(2)
    for zl in range(4)
    for c in range(2)
]
COLUMNS = [
    [linear(zh, x, zl, y, c) for zh in range(2) for zl in range(4)]
    for x in range(4)
    for y in range(4)
    for c in range(2)
]
CHANNELS = np.array(
    [
        6 * linear(zh, 2 * half, zl, y, 0) + k
        for y in range(4)
        for half in range(2)
        for zh in range(2)
        for zl in range(4)
        for k in range(6)
    ],
    dtype=np.int32,
).reshape(QUARTER, 1)


def dot(a, b, da, db):
    return lax.dot_general(a, b, (((da,), (db,)), ((), ())), preferred_element_type=F32)


def cumulative(values):
    return 0.5 * (1.0 + lax.erf(values * INVERSE_ROOT_TWO))


def gelu_value(values):
    return values * cumulative(values)


def gelu_slope(values):
    return cumulative(values) + values * jnp.exp(-0.5 * values * values) * INVERSE_ROOT_TAU


def reverser():
    rows = lax.broadcasted_iota(jnp.int32, (FLIP, FLIP), 0)
    cols = lax.broadcasted_iota(jnp.int32, (FLIP, FLIP), 1)
    return jnp.where(rows + cols == FLIP - 1, 1.0, 0.0).astype(BF)


def flip_channels(values, turn):
    parts = []
    for k in reversed(range(C // FLIP)):
        parts.append(dot(values[:, k * FLIP : (k + 1) * FLIP], turn, 1, 0).astype(BF))
    return jnp.concatenate(parts, axis=1)


def row_scale(wide):
    return lax.rsqrt(jnp.mean(wide * wide, axis=1, keepdims=True) + EPSILON)


def pool_inside(table, first_bin, rows):
    positions = first_bin + lax.broadcasted_iota(jnp.int32, (rows, table.shape[1]), 0)
    inside = (positions >= table[1:2, :]) & (positions < table[2:3, :])
    return jnp.where(inside, 1.0, 0.0).astype(BF)


def pool_member(table, genes):
    return jnp.where(genes == table[0:1, :], 1.0, 0.0).astype(BF)


def pack_kernel(position, head, tail, grads, out):
    odd = position[0] % 2
    edge = jnp.where(odd == 1, tail[...].astype(F32), head[...].astype(F32))
    rows = jnp.concatenate([grads[...].astype(F32), edge], axis=0).astype(BF)
    for seat in range(8):
        out[seat] = rows


def in_order(odd, own, partner):
    return jnp.where(odd == 0, own, partner), jnp.where(odd == 0, partner, own)


def normalized(wide):
    return (wide * row_scale(wide)).astype(BF)


def fetch(wc, taps, sems):
    copies = [pltpu.make_async_copy(wc.at[tap], taps.at[tap], sems.at[tap]) for tap in range(3)]
    for copy in copies:
        copy.start()
    return copies


def forward_kernel(position, tok, partner, wc, pre, taps, sems):
    copies = fetch(wc, taps, sems)
    low, high = in_order(position[0] % 2, tok[...].astype(F32), partner[...].astype(F32))
    normed = normalized(jnp.concatenate([low, high], axis=0))
    both = jnp.concatenate([normed, flip_channels(normed, reverser())], axis=0)
    rows = PAIR + 2 * DILATION
    edge = jnp.zeros((HALO, HID), F32)
    main = jnp.zeros((rows, HID), F32)
    mirror = jnp.zeros((rows, HID), F32)
    for tap in range(3):
        copies[tap].wait()
        product = dot(both, taps[tap], 1, 0)
        forth = jnp.concatenate([edge, product[0:PAIR], edge], axis=0)
        back = jnp.concatenate([edge, product[PAIR:], edge], axis=0)
        main = main + forth[tap * DILATION : tap * DILATION + rows]
        mirror = mirror + back[(2 - tap) * DILATION : (2 - tap) * DILATION + rows]
    pre[0, 0:rows] = main
    pre[1, 0:rows] = mirror
    pre[:, rows:ROWS] = jnp.zeros((2, ROWS - rows, HID), F32)


def slope_kernel(position, inner, wp, spread, table, wc, after, pre, gp, bin_grad, wide, taps, sems):
    del after
    copies = fetch(wc, taps, sems)
    turn = reverser()
    first = (position[0] // 2) * PAIR - DILATION
    row = lax.broadcasted_iota(jnp.int32, (128, table.shape[1]), 0)
    genes = jnp.where((row & 15) < 8, (row >> 4) * 8 + (row & 7), -1)
    inside = pool_inside(table[...], first, ROWS)
    counts = dot(inside, pool_member(table[...], genes), 1, 1).astype(BF)
    wide[...] = dot(counts, spread[...].reshape(128, C), 1, 0)
    covered = wide[...].astype(BF)
    own = pl.multiple_of((position[0] % 2) * BINS, BINS)
    bin_grad[...] = wide[pl.ds(own, BINS + 8)][DILATION : DILATION + BINS].astype(BF)
    both = jnp.concatenate([covered, flip_channels(covered, turn)], axis=0)
    grad_act = dot(both, wp[...], 1, 0)

    pair = position[0] // 2
    left = spread[jnp.maximum(2 * pair - 1, 0)][8 : 8 + HALO].astype(F32)
    right = spread[jnp.minimum(2 * pair + 2, 7)][8 : 8 + HALO].astype(F32)
    halo = jnp.concatenate([jnp.where(pair > 0, left, 0.0), jnp.where(pair < 3, right, 0.0)], axis=0)
    halo = normalized(halo)
    halo = jnp.concatenate([halo, flip_channels(halo, turn)], axis=0)
    rest = jnp.zeros((DILATION, HID), F32)
    sums = [jnp.zeros((HALO, HID), F32) for _ in range(4)]
    for tap in range(3):
        copies[tap].wait()
        product = dot(halo, taps[tap], 1, 0)
        for branch in range(2):
            left = product[2 * HALO * branch : 2 * HALO * branch + HALO]
            right = product[2 * HALO * branch + HALO : 2 * HALO * branch + 2 * HALO]
            shift = tap if branch == 0 else 2 - tap
            if shift == 0:
                sums[2 * branch] += left
            elif shift == 1:
                sums[2 * branch] += jnp.concatenate([left[DILATION:], rest], axis=0)
                sums[2 * branch + 1] += jnp.concatenate([rest, right[:DILATION]], axis=0)
            else:
                sums[2 * branch + 1] += right
    pre[...] = inner[...]
    for branch in range(2):
        pre[branch, 0:HALO] = pre[branch, 0:HALO] + sums[2 * branch]
        pre[branch, PAIR : PAIR + HALO] = pre[branch, PAIR : PAIR + HALO] + sums[2 * branch + 1]
    gp[0] = (grad_act[0:ROWS] * gelu_slope(pre[0])).astype(BF)
    gp[1] = (grad_act[ROWS:] * gelu_slope(pre[1])).astype(BF)


def turn_kernel(position, own, partner, channels, mine, others):
    odd = position[0] % 2
    low, high = in_order(odd, own[...].astype(F32), partner[...].astype(F32))
    normed = normalized(jnp.concatenate([low, high], axis=0))
    for out, core in ((mine, position[1]), (others, 1 - position[1])):
        wanted = channels[...] + 6 * odd + 48 * core
        main = jnp.zeros((QUARTER, PAIR), F32)
        mirror = jnp.zeros((QUARTER, PAIR), F32)
        for k in range(C // FLIP):
            lane = k * FLIP + lax.broadcasted_iota(jnp.int32, (QUARTER, FLIP), 1)
            piece = normed[:, k * FLIP : (k + 1) * FLIP]
            pick = jnp.where(lane == wanted, 1.0, 0.0).astype(BF)
            main = main + dot(pick, piece, 1, 1)
            pick = jnp.where(C - 1 - lane == wanted, 1.0, 0.0).astype(BF)
            mirror = mirror + dot(pick, piece, 1, 1)
        out[:, 0:PAIR] = main.astype(BF)
        out[:, PAIR:] = mirror.astype(BF)


def weight_kernel(turned, turned_other, own, other, out, done):
    done[...] = jnp.zeros((8, 128), F32)
    wide = [[ref[branch].astype(F32) for branch in range(2)] for ref in (own, other)]
    for tap in range(3):
        total = jnp.zeros((QUARTER, HID), F32)
        for ref, grads in zip((turned, turned_other), wide):
            main = grads[0][(2 - tap) * DILATION : (2 - tap) * DILATION + PAIR]
            mirror = grads[1][tap * DILATION : tap * DILATION + PAIR]
            total = total + dot(ref[...], jnp.concatenate([main, mirror], axis=0).astype(BF), 1, 0)
        out[:, tap] = (total * (1.0 / 32)).astype(BF).reshape(8, 48, HID)


def plane_sum_kernel(terms, out):
    total = terms[0].astype(F32)
    for k in range(1, 8):
        total = total + terms[k].astype(F32)
    for k in range(8):
        out[k] = total[:, 6 * k : 6 * k + 6].astype(BF)


def column_sum_kernel(terms, out):
    total = terms[0].astype(F32)
    for k in range(1, 8):
        total = total + terms[k].astype(F32)
    for tap in range(3):
        out[:, tap] = total[tap]


def output_kernel(position, tok, partner, pre, wp, table, give, keep):
    odd = position[0] % 2
    acts = [gelu_value(pre[branch][DILATION : DILATION + PAIR]).astype(BF) for branch in range(2)]
    outs = dot(jnp.concatenate(acts, axis=0), wp[...], 1, 1).astype(BF)
    mirror = flip_channels(outs[PAIR:], reverser())
    low, high = in_order(odd, tok[...].astype(F32), partner[...].astype(F32))
    block = jnp.concatenate([low, high], axis=0)
    block = (block + outs[0:PAIR].astype(F32) + mirror.astype(F32)).astype(BF)
    inside = pool_inside(table[...], (position[0] // 2) * PAIR, PAIR)
    row = lax.broadcasted_iota(jnp.int32, (GENES // 2, table.shape[1]), 0)
    genes = (row >> 3) * 16 + odd * 8 + (row & 7)
    counts = dot(pool_member(table[...], genes), inside, 1, 1).astype(BF)
    partial = dot(counts, block, 1, 0)
    low, high = partial[0 : GENES // 4], partial[GENES // 4 :]
    upper = position[0] // 4
    give[...] = jnp.where(upper == 0, high, low).astype(BF)
    keep[...] = jnp.where(upper == 0, low, high)


def input_kernel(position, tok, gp, bin_grad, wc, after, out, taps, sems):
    del after
    copies = fetch(wc, taps, sems)
    odd = position[0] % 2
    wide = tok[...].astype(F32)
    scale = row_scale(wide)
    unit = wide * scale
    turn = reverser()
    mirror_unit = flip_channels(tok[...], turn).astype(F32) * scale
    start = pl.multiple_of(odd * BINS, BINS)
    shifted = [gp[branch, pl.ds(start, BINS + 16)].astype(F32) for branch in range(2)]
    total = jnp.zeros((2 * BINS, C), F32)
    for tap in range(3):
        main = shifted[0][(2 - tap) * DILATION : (2 - tap) * DILATION + BINS]
        mirror = shifted[1][tap * DILATION : tap * DILATION + BINS]
        copies[tap].wait()
        total = total + dot(jnp.concatenate([main, mirror], axis=0).astype(BF), taps[tap], 1, 1)
    parts = []
    for grad, part in ((total[0:BINS], unit), (total[BINS:], mirror_unit)):
        centred = grad - part * jnp.mean(grad * part, axis=1, keepdims=True)
        parts.append((centred * scale).astype(BF))
    mirror = flip_channels(parts[1], turn)
    out[...] = (bin_grad[...].astype(F32) + parts[0].astype(F32) + mirror.astype(F32)).astype(BF)


def call(kernel, out_shape, *args, scalars=0, remote=(), scratch=(), work=1):
    specs = [pl.BlockSpec(memory_space=pltpu.SMEM)] * scalars
    for at in range(scalars, len(args)):
        specs.append(pl.BlockSpec(memory_space=pltpu.HBM if at in remote else pltpu.VMEM))
    return pl.pallas_call(
        kernel,
        out_shape=out_shape,
        in_specs=specs,
        scratch_shapes=scratch,
        cost_estimate=pl.CostEstimate(flops=int(work * 1e9), transcendentals=0, bytes_accessed=0),
        compiler_params=pltpu.CompilerParams(vmem_limit_bytes=VMEM_LIMIT),
    )(*args)


def pack(position, tok, grads):
    whole = lambda dims: pl.BlockSpec(dims, lambda i: (0,) * len(dims))
    return pl.pallas_call(
        pack_kernel,
        grid=(1,),
        out_shape=shape((8, 16, C), BF),
        in_specs=[
            pl.BlockSpec(memory_space=pltpu.SMEM),
            pl.BlockSpec((HALO, C), lambda i: (0, 0)),
            pl.BlockSpec((HALO, C), lambda i: (BINS // HALO - 1, 0)),
            whole((8, C)),
        ],
        out_specs=whole((8, 16, C)),
    )(position, tok, tok, grads)


DONE = jax.ShapeDtypeStruct((8, 128), F32)
FETCH = [pltpu.VMEM((3, C, HID), BF), pltpu.SemaphoreType.DMA((3,))]


def shape(dims, kind):
    return jax.ShapeDtypeStruct(dims, kind)


def scatter_genes(give, keep, seat):
    got = lax.ppermute(give, "seq", [(s, s ^ 4) for s in range(8)])
    values = keep + got.astype(F32)
    mine = (seat >> 1) & 1
    keep = jnp.where(mine == 0, values[:8], values[8:])
    give = jnp.where(mine == 0, values[8:], values[:8]).astype(BF)
    return keep + lax.ppermute(give, "seq", [(s, s ^ 2) for s in range(8)]).astype(F32)


def local(tokens, w_conv, w_point, exon_table, gene_grads):
    tok = tokens[0]
    table = exon_table[0]
    seat = lax.axis_index("seq").astype(jnp.int32)
    core = (lax.axis_index("batch") & 1).astype(jnp.int32)
    position = jnp.stack([seat, core])
    taps = pltpu.with_memory_space_constraint(jnp.transpose(w_conv, (1, 0, 2)), pltpu.HBM)

    partner = lax.ppermute(tok, "seq", SEQ_PAIRS)
    spread = pack(position, tok, gene_grads[0])
    spread = lax.all_to_all(spread, "seq", 0, 0, tiled=True)

    inner = call(
        forward_kernel,
        shape((2, ROWS, HID), F32),
        position,
        tok,
        partner,
        taps,
        work=FORWARD_WORK, scalars=1,
        remote=(3,),
        scratch=FETCH,
    )
    turned, lent = call(
        turn_kernel,
        (shape((QUARTER, 2 * PAIR), BF),) * 2,
        position,
        tok,
        partner,
        jnp.asarray(CHANNELS),
        work=TURN_WORK, scalars=1,
    )
    turned_other = lax.ppermute(lent, "batch", CORE_PAIRS)
    pre, gp, bin_grad = call(
        slope_kernel,
        (shape((2, ROWS, HID), F32), shape((2, ROWS, HID), BF), shape((BINS, C), BF)),
        position,
        inner,
        w_point,
        spread,
        table,
        taps,
        turned_other,
        work=SLOPE_WORK, scalars=1,
        remote=(5,),
        scratch=[pltpu.VMEM((ROWS, C), F32)] + FETCH,
    )
    gp_other = lax.ppermute(gp, "batch", CORE_PAIRS)
    terms, terms_done = call(
        weight_kernel, (shape((8, 3, 48, HID), BF), DONE), turned, turned_other, gp, gp_other
    )
    give, keep = call(
        output_kernel,
        (shape((GENES // 4, C), BF), shape((GENES // 4, C), F32)),
        position,
        tok,
        partner,
        pre,
        w_point,
        table,
        work=OUTPUT_WORK,
        scalars=1,
    )
    give, _ = lax.optimization_barrier((give, terms_done))
    pooled = scatter_genes(give, keep, seat)
    grad_input = call(
        input_kernel,
        shape((BINS, C), BF),
        position,
        tok,
        gp,
        bin_grad,
        taps,
        terms_done,
        work=INPUT_WORK, scalars=1,
        remote=(4,),
        scratch=FETCH,
    )
    terms = lax.all_to_all(terms, ("batch", "seq"), 0, 0, tiled=True, axis_index_groups=PLANES)
    terms = call(plane_sum_kernel, shape((8, 3, 6, HID), BF), terms, work=SUM_WORK)
    terms = lax.all_to_all(terms, ("batch", "seq"), 0, 0, tiled=True, axis_index_groups=COLUMNS)
    total = call(column_sum_kernel, shape((6, 3, HID), F32), terms, work=SUM_WORK)
    return (pooled[None], grad_input[None], total)


def solution(mesh):
    placed = (P("batch", "seq", None), P(), P(), P("batch", None, None), P("batch", "seq", None))
    return jax.shard_map(
        local,
        mesh=mesh,
        in_specs=placed,
        out_specs=(
            P("batch", "seq", None),
            P("batch", "seq", None),
            P(("batch", "seq"), None, None),
        ),
        check_vma=False,
    )
```

```python
import jax
import jax.numpy as jnp
import numpy as np
from jax import lax
from jax.experimental import pallas as pl
from jax.experimental.pallas import tpu as pltpu
from jax.sharding import PartitionSpec as P

DILATION = 4
GENES = 64
EXONS = 256
EPSILON = 1e-06
INVERSE_ROOT_TWO = 0.7071067811865476
INVERSE_ROOT_TAU = 0.3989422804014327

BINS = 128
PAIR = 2 * BINS
HALO = 8
ROWS = PAIR + 2 * HALO
C = 1536
HID = 384
QUARTER = C // 4
FLIP = 256
BF = jnp.bfloat16
F32 = jnp.float32
VMEM_LIMIT = 28 * 1024 * 1024

FORWARD_WORK = 0.5
SLOPE_WORK = 2
OUTPUT_WORK = 0.3
INPUT_WORK = 0.9
SUM_WORK = 1
CORE_PAIRS = [(b, b ^ 1) for b in range(32)]
SEQ_PAIRS = [(s, s ^ 1) for s in range(8)]


def linear(z_hi, x, z_lo, y, core):
    return ((z_lo * 4 + y) * 2 + core) * 8 + z_hi * 4 + x


PLANES = [
    [linear(zh, 2 * half + odd, zl, y, c) for y in range(4) for half in range(2)]
    for odd in range(2)
    for zh in range(2)
    for zl in range(4)
    for c in range(2)
]
COLUMNS = [
    [linear(zh, x, zl, y, c) for zh in range(2) for zl in range(4)]
    for x in range(4)
    for y in range(4)
    for c in range(2)
]
CHANNELS = np.array(
    [
        6 * linear(zh, 2 * half, zl, y, 0) + k
        for y in range(4)
        for half in range(2)
        for zh in range(2)
        for zl in range(4)
        for k in range(6)
    ],
    dtype=np.int32,
).reshape(QUARTER, 1)


def dot(a, b, da, db):
    return lax.dot_general(a, b, (((da,), (db,)), ((), ())), preferred_element_type=F32)


def cumulative(values):
    return 0.5 * (1.0 + lax.erf(values * INVERSE_ROOT_TWO))


def gelu_value(values):
    return values * cumulative(values)


def gelu_slope(values):
    return cumulative(values) + values * jnp.exp(-0.5 * values * values) * INVERSE_ROOT_TAU


def reverser():
    rows = lax.broadcasted_iota(jnp.int32, (FLIP, FLIP), 0)
    cols = lax.broadcasted_iota(jnp.int32, (FLIP, FLIP), 1)
    return jnp.where(rows + cols == FLIP - 1, 1.0, 0.0).astype(BF)


def flip_channels(values, turn):
    parts = []
    for k in reversed(range(C // FLIP)):
        parts.append(dot(values[:, k * FLIP : (k + 1) * FLIP], turn, 1, 0).astype(BF))
    return jnp.concatenate(parts, axis=1)


def row_scale(wide):
    return lax.rsqrt(jnp.mean(wide * wide, axis=1, keepdims=True) + EPSILON)


def pool_inside(table, first_bin, rows):
    positions = first_bin + lax.broadcasted_iota(jnp.int32, (rows, table.shape[1]), 0)
    inside = (positions >= table[1:2, :]) & (positions < table[2:3, :])
    return jnp.where(inside, 1.0, 0.0).astype(BF)


def pool_member(table, genes):
    return jnp.where(genes == table[0:1, :], 1.0, 0.0).astype(BF)


def seat():
    return lax.axis_index("seq").astype(jnp.int32)


def core():
    return lax.axis_index("batch").astype(jnp.int32) % 2


def pack_kernel(head, tail, grads, out):
    edge = jnp.where(seat() % 2 == 1, tail[...].astype(F32), head[...].astype(F32))
    out[...] = jnp.concatenate([grads[...].astype(F32), edge], axis=0).astype(BF)


def both_kernel(mine, across, out, done):
    upper = seat() // 4
    low, high = in_order(upper, mine[...].astype(F32), across[...].astype(F32))
    out[0] = low.astype(BF)
    out[1] = high.astype(BF)
    done[...] = jnp.zeros((8, 128), F32)


def in_order(odd, own, partner):
    return jnp.where(odd == 0, own, partner), jnp.where(odd == 0, partner, own)


def normalized(wide):
    return (wide * row_scale(wide)).astype(BF)


def turn(normed, channels, core_index, out):
    wanted = channels[...] + 6 * (seat() % 2) + 48 * core_index
    main = jnp.zeros((QUARTER, PAIR), F32)
    mirror = jnp.zeros((QUARTER, PAIR), F32)
    for k in range(C // FLIP):
        lane = k * FLIP + lax.broadcasted_iota(jnp.int32, (QUARTER, FLIP), 1)
        piece = normed[:, k * FLIP : (k + 1) * FLIP]
        pick = jnp.where(lane == wanted, 1.0, 0.0).astype(BF)
        main = main + dot(pick, piece, 1, 1)
        pick = jnp.where(C - 1 - lane == wanted, 1.0, 0.0).astype(BF)
        mirror = mirror + dot(pick, piece, 1, 1)
    out[:, 0:PAIR] = main.astype(BF)
    out[:, PAIR:] = mirror.astype(BF)


def forward_kernel(tok, partner, taps, channels, after, out, mine, others, pre, sem):
    del after
    low, high = in_order(seat() % 2, tok()[...].astype(F32), partner()[...].astype(F32))
    normed = normalized(jnp.concatenate([low, high], axis=0))
    both = jnp.concatenate([normed, flip_channels(normed, reverser())], axis=0)
    rows = PAIR + 2 * DILATION
    edge = jnp.zeros((HALO, HID), F32)
    main = jnp.zeros((rows, HID), F32)
    mirror = jnp.zeros((rows, HID), F32)
    for tap in range(3):
        product = dot(both, taps[tap]()[...], 1, 0)
        forth = jnp.concatenate([edge, product[0:PAIR], edge], axis=0)
        back = jnp.concatenate([edge, product[PAIR:], edge], axis=0)
        main = main + forth[tap * DILATION : tap * DILATION + rows]
        mirror = mirror + back[(2 - tap) * DILATION : (2 - tap) * DILATION + rows]
    pre[0, 0:rows] = main
    pre[1, 0:rows] = mirror
    pre[:, rows:ROWS] = jnp.zeros((2, ROWS - rows, HID), F32)
    copy = pltpu.make_async_copy(pre, out, sem)
    copy.start()
    turn(normed, channels(), 1 - core(), others)
    turn(normed, channels(), core(), mine)
    copy.wait()


def slope_kernel(s0, s1, s3, s2, table, wp, taps, inner, pre, gp, bin_grad, wide, spread):
    reverse = reverser()
    pair = seat() // 2
    odd = seat() % 2
    row = lax.broadcasted_iota(jnp.int32, (128, EXONS), 0)
    owner = ((row >> 4) & 1) * 4 + ((row >> 5) ^ (seat() & 3))
    genes = jnp.where((row & 15) < 8, owner * 8 + (row & 7), -1)
    table = table()[...]
    inside = pool_inside(table, pair * PAIR - DILATION, ROWS)
    counts = dot(inside, pool_member(table, genes), 1, 1).astype(BF)
    for apart, piece in enumerate((s0, s1, s2, s3)):
        spread[apart] = piece()[...]
    wide[...] = dot(counts, spread[...].reshape(128, C), 1, 0)
    covered = wide[...].astype(BF)
    own = pl.multiple_of(odd * BINS, BINS)
    bin_grad[...] = wide[pl.ds(own, BINS + 8)][DILATION : DILATION + BINS].astype(BF)
    both = jnp.concatenate([covered, flip_channels(covered, reverse)], axis=0)
    grad_act = dot(both, wp()[...], 1, 0)

    before = jnp.maximum(2 * pair - 1, 0)
    beyond = jnp.minimum(2 * pair + 2, 7)
    left = spread[(before ^ seat()) & 3, before // 4][8 : 8 + HALO].astype(F32)
    right = spread[(beyond ^ seat()) & 3, beyond // 4][8 : 8 + HALO].astype(F32)
    halo = jnp.concatenate([jnp.where(pair > 0, left, 0.0), jnp.where(pair < 3, right, 0.0)], axis=0)
    halo = normalized(halo)
    halo = jnp.concatenate([halo, flip_channels(halo, reverse)], axis=0)
    rest = jnp.zeros((DILATION, HID), F32)
    sums = [jnp.zeros((HALO, HID), F32) for _ in range(4)]
    for tap in range(3):
        product = dot(halo, taps[tap]()[...], 1, 0)
        for branch in range(2):
            left = product[2 * HALO * branch : 2 * HALO * branch + HALO]
            right = product[2 * HALO * branch + HALO : 2 * HALO * branch + 2 * HALO]
            shift = tap if branch == 0 else 2 - tap
            if shift == 0:
                sums[2 * branch] += left
            elif shift == 1:
                sums[2 * branch] += jnp.concatenate([left[DILATION:], rest], axis=0)
                sums[2 * branch + 1] += jnp.concatenate([rest, right[:DILATION]], axis=0)
            else:
                sums[2 * branch + 1] += right
    pre[...] = inner()[...]
    for branch in range(2):
        pre[branch, 0:HALO] = pre[branch, 0:HALO] + sums[2 * branch]
        pre[branch, PAIR : PAIR + HALO] = pre[branch, PAIR : PAIR + HALO] + sums[2 * branch + 1]
    gp[0] = (grad_act[0:ROWS] * gelu_slope(pre[0])).astype(BF)
    gp[1] = (grad_act[ROWS:] * gelu_slope(pre[1])).astype(BF)


def weight_kernel(turned, turned_other, own, other, out, done):
    done[...] = jnp.zeros((8, 128), F32)
    wide = [[ref()[branch].astype(F32) for branch in range(2)] for ref in (own, other)]
    for tap in range(3):
        total = jnp.zeros((QUARTER, HID), F32)
        for ref, grads in zip((turned, turned_other), wide):
            main = grads[0][(2 - tap) * DILATION : (2 - tap) * DILATION + PAIR]
            mirror = grads[1][tap * DILATION : tap * DILATION + PAIR]
            total = total + dot(ref()[...], jnp.concatenate([main, mirror], axis=0).astype(BF), 1, 0)
        out[:, tap] = (total * (1.0 / 32)).astype(BF).reshape(8, 48, HID)


def plane_sum_kernel(terms, out):
    total = terms[0].astype(F32)
    for k in range(1, 8):
        total = total + terms[k].astype(F32)
    for k in range(8):
        out[k] = total[:, 6 * k : 6 * k + 6].astype(BF)


def column_sum_kernel(terms, out):
    total = terms[0].astype(F32)
    for k in range(1, 8):
        total = total + terms[k].astype(F32)
    for tap in range(3):
        out[:, tap] = total[tap]


def output_kernel(tok, partner, pre, wp, table, give, keep):
    odd = seat() % 2
    pre = pre()
    acts = [gelu_value(pre[branch][DILATION : DILATION + PAIR]).astype(BF) for branch in range(2)]
    outs = dot(jnp.concatenate(acts, axis=0), wp()[...], 1, 1).astype(BF)
    mirror = flip_channels(outs[PAIR:], reverser())
    low, high = in_order(odd, tok()[...].astype(F32), partner()[...].astype(F32))
    block = jnp.concatenate([low, high], axis=0)
    block = (block + outs[0:PAIR].astype(F32) + mirror.astype(F32)).astype(BF)
    table = table()[...]
    inside = pool_inside(table, (seat() // 2) * PAIR, PAIR)
    row = lax.broadcasted_iota(jnp.int32, (GENES // 2, table.shape[1]), 0)
    genes = (row >> 3) * 16 + odd * 8 + (row & 7)
    counts = dot(pool_member(table, genes), inside, 1, 1).astype(BF)
    partial = dot(counts, block, 1, 0)
    low, high = partial[0 : GENES // 4], partial[GENES // 4 :]
    upper = seat() // 4
    give[...] = jnp.where(upper == 0, high, low).astype(BF)
    keep[...] = jnp.where(upper == 0, low, high)


def input_kernel(tok, gp, bin_grad, taps, after, out):
    del after
    odd = seat() % 2
    wide = tok()[...].astype(F32)
    scale = row_scale(wide)
    unit = wide * scale
    reverse = reverser()
    mirror_unit = flip_channels(tok()[...], reverse).astype(F32) * scale
    start = pl.multiple_of(odd * BINS, BINS)
    shifted = [gp()[branch, pl.ds(start, BINS + 16)].astype(F32) for branch in range(2)]
    total = jnp.zeros((2 * BINS, C), F32)
    for tap in range(3):
        main = shifted[0][(2 - tap) * DILATION : (2 - tap) * DILATION + BINS]
        mirror = shifted[1][tap * DILATION : tap * DILATION + BINS]
        total = total + dot(jnp.concatenate([main, mirror], axis=0).astype(BF), taps[tap]()[...], 1, 1)
    parts = []
    for grad, part in ((total[0:BINS], unit), (total[BINS:], mirror_unit)):
        centred = grad - part * jnp.mean(grad * part, axis=1, keepdims=True)
        parts.append((centred * scale).astype(BF))
    mirror = flip_channels(parts[1], reverse)
    out[...] = (bin_grad()[...].astype(F32) + parts[0].astype(F32) + mirror.astype(F32)).astype(BF)


def shape(dims, kind):
    return jax.ShapeDtypeStruct(dims, kind)


class Fetched:
    def __init__(self, source, buffer, sem):
        self.copy = pltpu.make_async_copy(source, buffer, sem)
        self.buffer = buffer
        self.waits = True
        self.copy.start()

    def __call__(self):
        if self.waits:
            self.copy.wait()
            self.waits = False
        return self.buffer


def call(kernel, out_shape, *args, order=(), large=(), far=(), pinned=False, scratch=(), work=1):
    outs = len(out_shape) if isinstance(out_shape, tuple) else 1
    places = [pl.BlockSpec(memory_space=pltpu.HBM if at in far else None) for at in range(outs)]
    count = len(args)
    if pinned:
        specs = [pl.BlockSpec(memory_space=pltpu.VMEM)] * count
        body, buffers = kernel, []
    else:
        args = list(args)
        specs = [pl.BlockSpec(memory_space=pl.ANY)] * count
        for at in large:
            specs[at] = pl.BlockSpec(memory_space=pltpu.HBM)
            args[at] = pltpu.with_memory_space_constraint(args[at], pltpu.HBM)
        fetched = [at for at in range(count) if at not in order]
        tapped = [at for at in fetched if args[at].shape == (3, C, HID)]
        buffers = [pltpu.VMEM(args[at].shape, args[at].dtype) for at in fetched]
        buffers.append(pltpu.SemaphoreType.DMA((len(fetched) + 2,)))

        def body(*refs):
            values = list(refs[:count])
            held = refs[count + outs : count + outs + len(fetched)]
            sems = refs[count + outs + len(fetched)]
            for k, at in enumerate(fetched):
                if at in tapped:
                    lanes = [k, len(fetched), len(fetched) + 1]
                    values[at] = [
                        Fetched(refs[at].at[tap], held[k].at[tap], sems.at[lanes[tap]])
                        for tap in range(3)
                    ]
                else:
                    values[at] = Fetched(refs[at], held[k], sems.at[k])
            kernel(*values, *refs[count : count + outs], *refs[count + outs + len(fetched) + 1 :])

    return pl.pallas_call(
        body,
        out_shape=out_shape,
        in_specs=specs,
        out_specs=tuple(places) if isinstance(out_shape, tuple) else places[0],
        scratch_shapes=buffers + list(scratch),
        cost_estimate=pl.CostEstimate(flops=int(work * 1e9), transcendentals=0, bytes_accessed=0),
        compiler_params=pltpu.CompilerParams(vmem_limit_bytes=VMEM_LIMIT),
    )(*args)


def pack(tok, grads):
    return pl.pallas_call(
        pack_kernel,
        grid=(1,),
        out_shape=shape((16, C), BF),
        in_specs=[
            pl.BlockSpec((HALO, C), lambda i: (0, 0)),
            pl.BlockSpec((HALO, C), lambda i: (BINS // HALO - 1, 0)),
            pl.BlockSpec((8, C), lambda i: (0, 0)),
        ],
        out_specs=pl.BlockSpec((16, C), lambda i: (0, 0)),
    )(tok, tok, grads)


DONE = jax.ShapeDtypeStruct((8, 128), F32)


def scatter_genes(give, keep):
    got = lax.ppermute(give, "seq", [(s, s ^ 4) for s in range(8)])
    values = keep + got.astype(F32)
    mine = (seat() >> 1) & 1
    keep = jnp.where(mine == 0, values[:8], values[8:])
    give = jnp.where(mine == 0, values[8:], values[:8]).astype(BF)
    return keep + lax.ppermute(give, "seq", [(s, s ^ 2) for s in range(8)]).astype(F32)


def local(tokens, w_conv, w_point, exon_table, gene_grads):
    tok = tokens[0]
    table = exon_table[0]
    taps = jnp.transpose(w_conv, (1, 0, 2))
    pair_rows = shape((2, ROWS, HID), F32)

    partner = lax.ppermute(tok, "seq", SEQ_PAIRS)
    mine = pack(tok, gene_grads[0])
    across = lax.ppermute(mine, "seq", [(s, s ^ 4) for s in range(8)])
    both, ready = call(
        both_kernel, (shape((2, 16, C), BF), DONE), mine, across, pinned=True, work=SUM_WORK
    )
    spread = [both]
    for apart in (1, 3, 2):
        spread.append(lax.ppermute(both, "seq", [(s, s ^ apart) for s in range(8)]))

    quarter = shape((QUARTER, 2 * PAIR), BF)
    inner, turned, lent = call(
        forward_kernel,
        (pair_rows, quarter, quarter),
        tok,
        partner,
        taps,
        jnp.asarray(CHANNELS),
        ready,
        large=(0, 2),
        order=(4,),
        far=(0,),
        scratch=[pltpu.VMEM((2, ROWS, HID), F32), pltpu.SemaphoreType.DMA],
        work=FORWARD_WORK,
    )
    turned_other = lax.ppermute(lent, "batch", CORE_PAIRS)
    pre, gp, bin_grad = call(
        slope_kernel,
        (pair_rows, shape((2, ROWS, HID), BF), shape((BINS, C), BF)),
        *spread,
        table,
        w_point,
        taps,
        inner,
        large=(5, 6),
        work=SLOPE_WORK,
        scratch=[pltpu.VMEM((ROWS, C), F32), pltpu.VMEM((4, 2, 16, C), BF)],
    )
    gp_other = lax.ppermute(gp, "batch", CORE_PAIRS)
    terms, terms_done = call(
        weight_kernel, (shape((8, 3, 48, HID), BF), DONE), turned, turned_other, gp, gp_other
    )
    give, keep = call(
        output_kernel,
        (shape((GENES // 4, C), BF), shape((GENES // 4, C), F32)),
        tok,
        partner,
        pre,
        w_point,
        table,
        large=(0, 3),
        work=OUTPUT_WORK,
    )
    give, _ = lax.optimization_barrier((give, terms_done))
    pooled = scatter_genes(give, keep)
    grad_input = call(
        input_kernel,
        shape((BINS, C), BF),
        tok,
        gp,
        bin_grad,
        taps,
        terms_done,
        large=(0, 3),
        order=(4,),
        work=INPUT_WORK,
    )
    terms = lax.all_to_all(terms, ("batch", "seq"), 0, 0, tiled=True, axis_index_groups=PLANES)
    terms = call(plane_sum_kernel, shape((8, 3, 6, HID), BF), terms, pinned=True, work=SUM_WORK)
    terms = lax.all_to_all(terms, ("batch", "seq"), 0, 0, tiled=True, axis_index_groups=COLUMNS)
    total = call(column_sum_kernel, shape((6, 3, HID), F32), terms, pinned=True, work=SUM_WORK)
    return (pooled[None], grad_input[None], total)


def solution(mesh):
    placed = (P("batch", "seq", None), P(), P(), P("batch", None, None), P("batch", "seq", None))
    return jax.shard_map(
        local,
        mesh=mesh,
        in_specs=placed,
        out_specs=(
            P("batch", "seq", None),
            P("batch", "seq", None),
            P(("batch", "seq"), None, None),
        ),
        check_vma=False,
    )
```

```python
import jax
import jax.numpy as jnp
import numpy as np
from jax import lax
from jax.experimental import pallas as pl
from jax.experimental.pallas import tpu as pltpu
from jax.sharding import PartitionSpec as P

DILATION = 4
GENES = 64
EXONS = 256
EPSILON = 1e-06
INVERSE_ROOT_TWO = 0.7071067811865476
INVERSE_ROOT_TAU = 0.3989422804014327

BINS = 128
PAIR = 2 * BINS
HALO = 8
ROWS = PAIR + 2 * HALO
C = 1536
HID = 384
QUARTER = C // 4
FLIP = 256
BF = jnp.bfloat16
F32 = jnp.float32
VMEM_LIMIT = 28 * 1024 * 1024

FORWARD_WORK = 4
SLOPE_WORK = 2
TURN_WORK = 1
OUTPUT_WORK = 0.3
INPUT_WORK = 0.4
SUM_WORK = 1
CORE_PAIRS = [(b, b ^ 1) for b in range(32)]
SEQ_PAIRS = [(s, s ^ 1) for s in range(8)]


def linear(z_hi, x, z_lo, y, core):
    return ((z_lo * 4 + y) * 2 + core) * 8 + z_hi * 4 + x


PLANES = [
    [linear(zh, 2 * half + odd, zl, y, c) for y in range(4) for half in range(2)]
    for odd in range(2)
    for zh in range(2)
    for zl in range(4)
    for c in range(2)
]
COLUMNS = [
    [linear(zh, x, zl, y, c) for zh in range(2) for zl in range(4)]
    for x in range(4)
    for y in range(4)
    for c in range(2)
]
CHANNELS = np.array(
    [
        6 * linear(zh, 2 * half, zl, y, 0) + k
        for y in range(4)
        for half in range(2)
        for zh in range(2)
        for zl in range(4)
        for k in range(6)
    ],
    dtype=np.int32,
).reshape(QUARTER, 1)


def dot(a, b, da, db):
    return lax.dot_general(a, b, (((da,), (db,)), ((), ())), preferred_element_type=F32)


def cumulative(values):
    return 0.5 * (1.0 + lax.erf(values * INVERSE_ROOT_TWO))


def gelu_value(values):
    return values * cumulative(values)


def gelu_slope(values):
    return cumulative(values) + values * jnp.exp(-0.5 * values * values) * INVERSE_ROOT_TAU


def reverser():
    rows = lax.broadcasted_iota(jnp.int32, (FLIP, FLIP), 0)
    cols = lax.broadcasted_iota(jnp.int32, (FLIP, FLIP), 1)
    return jnp.where(rows + cols == FLIP - 1, 1.0, 0.0).astype(BF)


def flip_channels(values, turn):
    parts = []
    for k in reversed(range(C // FLIP)):
        parts.append(dot(values[:, k * FLIP : (k + 1) * FLIP], turn, 1, 0).astype(BF))
    return jnp.concatenate(parts, axis=1)


def row_scale(wide):
    return lax.rsqrt(jnp.mean(wide * wide, axis=1, keepdims=True) + EPSILON)


def pool_inside(table, first_bin, rows):
    positions = first_bin + lax.broadcasted_iota(jnp.int32, (rows, table.shape[1]), 0)
    inside = (positions >= table[1:2, :]) & (positions < table[2:3, :])
    return jnp.where(inside, 1.0, 0.0).astype(BF)


def pool_member(table, genes):
    return jnp.where(genes == table[0:1, :], 1.0, 0.0).astype(BF)


def seat():
    return lax.axis_index("seq").astype(jnp.int32)


def core():
    return lax.axis_index("batch").astype(jnp.int32) % 2


def pack_kernel(head, tail, grads, out):
    edge = jnp.where(seat() % 2 == 1, tail[...].astype(F32), head[...].astype(F32))
    out[...] = jnp.concatenate([grads[...].astype(F32), edge], axis=0).astype(BF)


def both_kernel(mine, across, out, done):
    upper = seat() // 4
    low, high = in_order(upper, mine[...].astype(F32), across[...].astype(F32))
    out[0] = low.astype(BF)
    out[1] = high.astype(BF)
    done[...] = jnp.zeros((8, 128), F32)


def in_order(odd, own, partner):
    return jnp.where(odd == 0, own, partner), jnp.where(odd == 0, partner, own)


def normalized(wide):
    return (wide * row_scale(wide)).astype(BF)


def turn(normed, channels, out):
    wanted = channels[...] + 6 * (seat() % 2) + 48 * core()
    main = jnp.zeros((QUARTER, PAIR), F32)
    mirror = jnp.zeros((QUARTER, PAIR), F32)
    for k in range(C // FLIP):
        lane = k * FLIP + lax.broadcasted_iota(jnp.int32, (QUARTER, FLIP), 1)
        piece = normed[:, k * FLIP : (k + 1) * FLIP]
        pick = jnp.where(lane == wanted, 1.0, 0.0).astype(BF)
        main = main + dot(pick, piece, 1, 1)
        pick = jnp.where(C - 1 - lane == wanted, 1.0, 0.0).astype(BF)
        mirror = mirror + dot(pick, piece, 1, 1)
    out[:, 0:PAIR] = main.astype(BF)
    out[:, PAIR:] = mirror.astype(BF)


def turn_kernel(own, partner, other, other_partner, channels, after, mine, others):
    del after
    odd = seat() % 2
    for low, high, out in ((own, partner, mine), (other, other_partner, others)):
        low, high = in_order(odd, low()[...].astype(F32), high()[...].astype(F32))
        turn(normalized(jnp.concatenate([low, high], axis=0)), channels(), out)


def forward_kernel(tok, partner, taps, after, out, pre, sem):
    del after
    low, high = in_order(seat() % 2, tok()[...].astype(F32), partner()[...].astype(F32))
    normed = normalized(jnp.concatenate([low, high], axis=0))
    both = jnp.concatenate([normed, flip_channels(normed, reverser())], axis=0)
    rows = PAIR + 2 * DILATION
    edge = jnp.zeros((HALO, HID), F32)
    main = jnp.zeros((rows, HID), F32)
    mirror = jnp.zeros((rows, HID), F32)
    for tap in range(3):
        product = dot(both, taps[tap]()[...], 1, 0)
        forth = jnp.concatenate([edge, product[0:PAIR], edge], axis=0)
        back = jnp.concatenate([edge, product[PAIR:], edge], axis=0)
        main = main + forth[tap * DILATION : tap * DILATION + rows]
        mirror = mirror + back[(2 - tap) * DILATION : (2 - tap) * DILATION + rows]
    pre[0, 0:rows] = main
    pre[1, 0:rows] = mirror
    pre[:, rows:ROWS] = jnp.zeros((2, ROWS - rows, HID), F32)
    copy = pltpu.make_async_copy(pre, out, sem)
    copy.start()
    copy.wait()


def slope_kernel(s0, s1, s3, s2, table, wp, taps, inner, pre, gp, bin_grad, done, wide, spread):
    done[...] = jnp.zeros((8, 128), F32)
    reverse = reverser()
    pair = seat() // 2
    odd = seat() % 2
    row = lax.broadcasted_iota(jnp.int32, (128, EXONS), 0)
    owner = ((row >> 4) & 1) * 4 + ((row >> 5) ^ (seat() & 3))
    genes = jnp.where((row & 15) < 8, owner * 8 + (row & 7), -1)
    table = table()[...]
    inside = pool_inside(table, pair * PAIR - DILATION, ROWS)
    counts = dot(inside, pool_member(table, genes), 1, 1).astype(BF)
    for apart, piece in enumerate((s0, s1, s2, s3)):
        spread[apart] = piece()[...]
    wide[...] = dot(counts, spread[...].reshape(128, C), 1, 0)
    covered = wide[...].astype(BF)
    own = pl.multiple_of(odd * BINS, BINS)
    bin_grad[...] = wide[pl.ds(own, BINS + 8)][DILATION : DILATION + BINS].astype(BF)
    both = jnp.concatenate([covered, flip_channels(covered, reverse)], axis=0)
    grad_act = dot(both, wp()[...], 1, 0)

    before = jnp.maximum(2 * pair - 1, 0)
    beyond = jnp.minimum(2 * pair + 2, 7)
    left = spread[(before ^ seat()) & 3, before // 4][8 : 8 + HALO].astype(F32)
    right = spread[(beyond ^ seat()) & 3, beyond // 4][8 : 8 + HALO].astype(F32)
    halo = jnp.concatenate([jnp.where(pair > 0, left, 0.0), jnp.where(pair < 3, right, 0.0)], axis=0)
    halo = normalized(halo)
    halo = jnp.concatenate([halo, flip_channels(halo, reverse)], axis=0)
    rest = jnp.zeros((DILATION, HID), F32)
    sums = [jnp.zeros((HALO, HID), F32) for _ in range(4)]
    for tap in range(3):
        product = dot(halo, taps[tap]()[...], 1, 0)
        for branch in range(2):
            left = product[2 * HALO * branch : 2 * HALO * branch + HALO]
            right = product[2 * HALO * branch + HALO : 2 * HALO * branch + 2 * HALO]
            shift = tap if branch == 0 else 2 - tap
            if shift == 0:
                sums[2 * branch] += left
            elif shift == 1:
                sums[2 * branch] += jnp.concatenate([left[DILATION:], rest], axis=0)
                sums[2 * branch + 1] += jnp.concatenate([rest, right[:DILATION]], axis=0)
            else:
                sums[2 * branch + 1] += right
    pre[...] = inner()[...]
    for branch in range(2):
        pre[branch, 0:HALO] = pre[branch, 0:HALO] + sums[2 * branch]
        pre[branch, PAIR : PAIR + HALO] = pre[branch, PAIR : PAIR + HALO] + sums[2 * branch + 1]
    gp[0] = (grad_act[0:ROWS] * gelu_slope(pre[0])).astype(BF)
    gp[1] = (grad_act[ROWS:] * gelu_slope(pre[1])).astype(BF)


def weight_kernel(turned, turned_other, own, other, out, done):
    done[...] = jnp.zeros((8, 128), F32)
    wide = [[ref()[branch].astype(F32) for branch in range(2)] for ref in (own, other)]
    for tap in range(3):
        total = jnp.zeros((QUARTER, HID), F32)
        for ref, grads in zip((turned, turned_other), wide):
            main = grads[0][(2 - tap) * DILATION : (2 - tap) * DILATION + PAIR]
            mirror = grads[1][tap * DILATION : tap * DILATION + PAIR]
            total = total + dot(ref()[...], jnp.concatenate([main, mirror], axis=0).astype(BF), 1, 0)
        out[:, tap] = (total * (1.0 / 32)).astype(BF).reshape(8, 48, HID)


def plane_sum_kernel(terms, out):
    total = terms[0].astype(F32)
    for k in range(1, 8):
        total = total + terms[k].astype(F32)
    for k in range(8):
        out[k] = total[:, 6 * k : 6 * k + 6].astype(BF)


def column_sum_kernel(terms, out):
    total = terms[0].astype(F32)
    for k in range(1, 8):
        total = total + terms[k].astype(F32)
    for tap in range(3):
        out[:, tap] = total[tap]


def output_kernel(tok, partner, pre, wp, table, give, keep):
    odd = seat() % 2
    pre = pre()
    acts = [gelu_value(pre[branch][DILATION : DILATION + PAIR]).astype(BF) for branch in range(2)]
    outs = dot(jnp.concatenate(acts, axis=0), wp()[...], 1, 1).astype(BF)
    mirror = flip_channels(outs[PAIR:], reverser())
    low, high = in_order(odd, tok()[...].astype(F32), partner()[...].astype(F32))
    block = jnp.concatenate([low, high], axis=0)
    block = (block + outs[0:PAIR].astype(F32) + mirror.astype(F32)).astype(BF)
    table = table()[...]
    inside = pool_inside(table, (seat() // 2) * PAIR, PAIR)
    row = lax.broadcasted_iota(jnp.int32, (GENES // 2, table.shape[1]), 0)
    genes = (row >> 3) * 16 + odd * 8 + (row & 7)
    counts = dot(pool_member(table, genes), inside, 1, 1).astype(BF)
    partial = dot(counts, block, 1, 0)
    half = (seat() // 2) % 2
    low = jnp.concatenate([partial[0:8], partial[16:24]], axis=0)
    high = jnp.concatenate([partial[8:16], partial[24:32]], axis=0)
    give[...] = jnp.where(half == 0, high, low).astype(BF)
    keep[...] = jnp.where(half == 0, low, high)


def input_kernel(tok, gp, bin_grad, taps, got, mine, after, out, give, keep):
    del after
    sums = mine()[...] + got()[...].astype(F32)
    upper = seat() // 4
    give[...] = jnp.where(upper == 0, sums[8:], sums[:8]).astype(BF)
    keep[...] = jnp.where(upper == 0, sums[:8], sums[8:])
    odd = seat() % 2
    wide = tok()[...].astype(F32)
    scale = row_scale(wide)
    unit = wide * scale
    reverse = reverser()
    mirror_unit = flip_channels(tok()[...], reverse).astype(F32) * scale
    start = pl.multiple_of(odd * BINS, BINS)
    shifted = [gp()[branch, pl.ds(start, BINS + 16)].astype(F32) for branch in range(2)]
    total = jnp.zeros((2 * BINS, C), F32)
    for tap in range(3):
        main = shifted[0][(2 - tap) * DILATION : (2 - tap) * DILATION + BINS]
        mirror = shifted[1][tap * DILATION : tap * DILATION + BINS]
        total = total + dot(jnp.concatenate([main, mirror], axis=0).astype(BF), taps[tap]()[...], 1, 1)
    parts = []
    for grad, part in ((total[0:BINS], unit), (total[BINS:], mirror_unit)):
        centred = grad - part * jnp.mean(grad * part, axis=1, keepdims=True)
        parts.append((centred * scale).astype(BF))
    mirror = flip_channels(parts[1], reverse)
    out[...] = (bin_grad()[...].astype(F32) + parts[0].astype(F32) + mirror.astype(F32)).astype(BF)


def shape(dims, kind):
    return jax.ShapeDtypeStruct(dims, kind)


class Fetched:
    def __init__(self, source, buffer, sem):
        self.copy = pltpu.make_async_copy(source, buffer, sem)
        self.buffer = buffer
        self.waits = True
        self.copy.start()

    def __call__(self):
        if self.waits:
            self.copy.wait()
            self.waits = False
        return self.buffer


def call(kernel, out_shape, *args, order=(), large=(), far=(), pinned=False, scratch=(), work=1):
    outs = len(out_shape) if isinstance(out_shape, tuple) else 1
    places = [pl.BlockSpec(memory_space=pltpu.HBM if at in far else None) for at in range(outs)]
    count = len(args)
    if pinned:
        specs = [pl.BlockSpec(memory_space=pltpu.VMEM)] * count
        body, buffers = kernel, []
    else:
        args = list(args)
        specs = [pl.BlockSpec(memory_space=pl.ANY)] * count
        for at in large:
            specs[at] = pl.BlockSpec(memory_space=pltpu.HBM)
            args[at] = pltpu.with_memory_space_constraint(args[at], pltpu.HBM)
        fetched = [at for at in range(count) if at not in order]
        tapped = [at for at in fetched if args[at].shape == (3, C, HID)]
        buffers = [pltpu.VMEM(args[at].shape, args[at].dtype) for at in fetched]
        buffers.append(pltpu.SemaphoreType.DMA((len(fetched) + 2,)))

        def body(*refs):
            values = list(refs[:count])
            held = refs[count + outs : count + outs + len(fetched)]
            sems = refs[count + outs + len(fetched)]
            for k, at in enumerate(fetched):
                if at in tapped:
                    lanes = [k, len(fetched), len(fetched) + 1]
                    values[at] = [
                        Fetched(refs[at].at[tap], held[k].at[tap], sems.at[lanes[tap]])
                        for tap in range(3)
                    ]
                else:
                    values[at] = Fetched(refs[at], held[k], sems.at[k])
            kernel(*values, *refs[count : count + outs], *refs[count + outs + len(fetched) + 1 :])

    return pl.pallas_call(
        body,
        out_shape=out_shape,
        in_specs=specs,
        out_specs=tuple(places) if isinstance(out_shape, tuple) else places[0],
        scratch_shapes=buffers + list(scratch),
        cost_estimate=pl.CostEstimate(flops=int(work * 1e9), transcendentals=0, bytes_accessed=0),
        compiler_params=pltpu.CompilerParams(vmem_limit_bytes=VMEM_LIMIT),
    )(*args)


def pack(tok, grads):
    return pl.pallas_call(
        pack_kernel,
        grid=(1,),
        out_shape=shape((16, C), BF),
        in_specs=[
            pl.BlockSpec((HALO, C), lambda i: (0, 0)),
            pl.BlockSpec((HALO, C), lambda i: (BINS // HALO - 1, 0)),
            pl.BlockSpec((8, C), lambda i: (0, 0)),
        ],
        out_specs=pl.BlockSpec((16, C), lambda i: (0, 0)),
    )(tok, tok, grads)


DONE = jax.ShapeDtypeStruct((8, 128), F32)


def local(tokens, w_conv, w_point, exon_table, gene_grads):
    tok = tokens[0]
    table = exon_table[0]
    taps = jnp.transpose(w_conv, (1, 0, 2))
    pair_rows = shape((2, ROWS, HID), F32)

    partner = lax.ppermute(tok, "seq", SEQ_PAIRS)
    other = lax.ppermute(tok, "batch", CORE_PAIRS)
    other_partner = lax.ppermute(partner, "batch", CORE_PAIRS)
    mine = pack(tok, gene_grads[0])
    across = lax.ppermute(mine, "seq", [(s, s ^ 4) for s in range(8)])
    both, ready = call(
        both_kernel, (shape((2, 16, C), BF), DONE), mine, across, pinned=True, work=SUM_WORK
    )
    spread = [both]
    for apart in (1, 3, 2):
        spread.append(lax.ppermute(both, "seq", [(s, s ^ apart) for s in range(8)]))

    (inner,) = call(
        forward_kernel,
        (pair_rows,),
        tok,
        partner,
        taps,
        ready,
        large=(0, 2),
        order=(3,),
        far=(0,),
        scratch=[pltpu.VMEM((2, ROWS, HID), F32), pltpu.SemaphoreType.DMA],
        work=FORWARD_WORK,
    )
    pre, gp, bin_grad, slope_done = call(
        slope_kernel,
        (pair_rows, shape((2, ROWS, HID), BF), shape((BINS, C), BF), DONE),
        *spread,
        table,
        w_point,
        taps,
        inner,
        large=(5, 6),
        work=SLOPE_WORK,
        scratch=[pltpu.VMEM((ROWS, C), F32), pltpu.VMEM((4, 2, 16, C), BF)],
    )
    gp_other = lax.ppermute(gp, "batch", CORE_PAIRS)
    quarter = shape((QUARTER, 2 * PAIR), BF)
    turned, turned_other = call(
        turn_kernel,
        (quarter, quarter),
        tok,
        partner,
        other,
        other_partner,
        jnp.asarray(CHANNELS),
        slope_done,
        large=(0,),
        order=(5,),
        work=TURN_WORK,
    )
    terms, terms_done = call(
        weight_kernel, (shape((8, 3, 48, HID), BF), DONE), turned, turned_other, gp, gp_other
    )
    give, keep = call(
        output_kernel,
        (shape((GENES // 4, C), BF), shape((GENES // 4, C), F32)),
        tok,
        partner,
        pre,
        w_point,
        table,
        large=(0, 3),
        work=OUTPUT_WORK,
    )
    got = lax.ppermute(give, "seq", [(s, s ^ 2) for s in range(8)])
    grad_input, give, keep = call(
        input_kernel,
        (shape((BINS, C), BF), shape((GENES // 8, C), BF), shape((GENES // 8, C), F32)),
        tok,
        gp,
        bin_grad,
        taps,
        got,
        keep,
        terms_done,
        large=(0, 3),
        order=(6,),
        work=INPUT_WORK,
    )
    pooled = keep + lax.ppermute(give, "seq", [(s, s ^ 4) for s in range(8)]).astype(F32)
    terms = lax.all_to_all(terms, ("batch", "seq"), 0, 0, tiled=True, axis_index_groups=PLANES)
    terms = call(plane_sum_kernel, shape((8, 3, 6, HID), BF), terms, pinned=True, work=SUM_WORK)
    terms = lax.all_to_all(terms, ("batch", "seq"), 0, 0, tiled=True, axis_index_groups=COLUMNS)
    total = call(column_sum_kernel, shape((6, 3, HID), F32), terms, pinned=True, work=SUM_WORK)
    return (pooled[None], grad_input[None], total)


def solution(mesh):
    placed = (P("batch", "seq", None), P(), P(), P("batch", None, None), P("batch", "seq", None))
    return jax.shard_map(
        local,
        mesh=mesh,
        in_specs=placed,
        out_specs=(
            P("batch", "seq", None),
            P("batch", "seq", None),
            P(("batch", "seq"), None, None),
        ),
        check_vma=False,
    )
```

```python
import jax
import jax.numpy as jnp
import numpy as np
from jax import lax
from jax.experimental import pallas as pl
from jax.experimental.pallas import tpu as pltpu
from jax.sharding import PartitionSpec as P

DILATION = 4
GENES = 64
EXONS = 256
EPSILON = 1e-06
INVERSE_ROOT_TWO = 0.7071067811865476
INVERSE_ROOT_TAU = 0.3989422804014327

BINS = 128
PAIR = 2 * BINS
HALO = 8
ROWS = PAIR + 2 * HALO
C = 1536
HID = 384
QUARTER = C // 4
FLIP = 256
BF = jnp.bfloat16
F32 = jnp.float32
VMEM_LIMIT = 28 * 1024 * 1024

FORWARD_WORK = 0.5
SLOPE_WORK = 2
OUTPUT_WORK = 0.3
INPUT_WORK = 0.9
SUM_WORK = 1
CORE_PAIRS = [(b, b ^ 1) for b in range(32)]
SEQ_PAIRS = [(s, s ^ 1) for s in range(8)]


def linear(z_hi, x, z_lo, y, core):
    return ((z_lo * 4 + y) * 2 + core) * 8 + z_hi * 4 + x


PLANES = [
    [linear(zh, 2 * half + odd, zl, y, c) for y in range(4) for half in range(2)]
    for odd in range(2)
    for zh in range(2)
    for zl in range(4)
    for c in range(2)
]
COLUMNS = [
    [linear(zh, x, zl, y, c) for zh in range(2) for zl in range(4)]
    for x in range(4)
    for y in range(4)
    for c in range(2)
]
CHANNELS = np.array(
    [
        6 * linear(zh, 2 * half, zl, y, 0) + k
        for y in range(4)
        for half in range(2)
        for zh in range(2)
        for zl in range(4)
        for k in range(6)
    ],
    dtype=np.int32,
).reshape(QUARTER, 1)


def dot(a, b, da, db):
    return lax.dot_general(a, b, (((da,), (db,)), ((), ())), preferred_element_type=F32)


def cumulative(values):
    return 0.5 * (1.0 + lax.erf(values * INVERSE_ROOT_TWO))


def gelu_value(values):
    return values * cumulative(values)


def gelu_slope(values):
    return cumulative(values) + values * jnp.exp(-0.5 * values * values) * INVERSE_ROOT_TAU


def reverser():
    rows = lax.broadcasted_iota(jnp.int32, (FLIP, FLIP), 0)
    cols = lax.broadcasted_iota(jnp.int32, (FLIP, FLIP), 1)
    return jnp.where(rows + cols == FLIP - 1, 1.0, 0.0).astype(BF)


def flip_channels(values, turn):
    parts = []
    for k in reversed(range(C // FLIP)):
        parts.append(dot(values[:, k * FLIP : (k + 1) * FLIP], turn, 1, 0).astype(BF))
    return jnp.concatenate(parts, axis=1)


def row_scale(wide):
    return lax.rsqrt(jnp.mean(wide * wide, axis=1, keepdims=True) + EPSILON)


def pool_inside(table, first_bin, rows):
    positions = first_bin + lax.broadcasted_iota(jnp.int32, (rows, table.shape[1]), 0)
    inside = (positions >= table[1:2, :]) & (positions < table[2:3, :])
    return jnp.where(inside, 1.0, 0.0).astype(BF)


def pool_member(table, genes):
    return jnp.where(genes == table[0:1, :], 1.0, 0.0).astype(BF)


def seat():
    return lax.axis_index("seq").astype(jnp.int32)


def core():
    return lax.axis_index("batch").astype(jnp.int32) % 2


def pack_kernel(head, tail, grads, out):
    edge = jnp.where(seat() % 2 == 1, tail[...].astype(F32), head[...].astype(F32))
    out[...] = jnp.concatenate([grads[...].astype(F32), edge], axis=0).astype(BF)


def both_kernel(mine, across, out, done):
    upper = seat() // 4
    low, high = in_order(upper, mine[...].astype(F32), across[...].astype(F32))
    out[0] = low.astype(BF)
    out[1] = high.astype(BF)
    done[...] = jnp.zeros((8, 128), F32)


def in_order(odd, own, partner):
    return jnp.where(odd == 0, own, partner), jnp.where(odd == 0, partner, own)


def normalized(wide):
    return (wide * row_scale(wide)).astype(BF)


def turn(normed, channels, core_index, out):
    wanted = channels[...] + 6 * (seat() % 2) + 48 * core_index
    main = jnp.zeros((QUARTER, PAIR), F32)
    mirror = jnp.zeros((QUARTER, PAIR), F32)
    for k in range(C // FLIP):
        lane = k * FLIP + lax.broadcasted_iota(jnp.int32, (QUARTER, FLIP), 1)
        piece = normed[:, k * FLIP : (k + 1) * FLIP]
        pick = jnp.where(lane == wanted, 1.0, 0.0).astype(BF)
        main = main + dot(pick, piece, 1, 1)
        pick = jnp.where(C - 1 - lane == wanted, 1.0, 0.0).astype(BF)
        mirror = mirror + dot(pick, piece, 1, 1)
    out[:, 0:PAIR] = main.astype(BF)
    out[:, PAIR:] = mirror.astype(BF)


def forward_kernel(tok, partner, taps, channels, after, out, mine, others, pre, sem):
    del after
    low, high = in_order(seat() % 2, tok()[...].astype(F32), partner()[...].astype(F32))
    normed = normalized(jnp.concatenate([low, high], axis=0))
    both = jnp.concatenate([normed, flip_channels(normed, reverser())], axis=0)
    rows = PAIR + 2 * DILATION
    edge = jnp.zeros((HALO, HID), F32)
    main = jnp.zeros((rows, HID), F32)
    mirror = jnp.zeros((rows, HID), F32)
    for tap in range(3):
        product = dot(both, taps[tap]()[...], 1, 0)
        forth = jnp.concatenate([edge, product[0:PAIR], edge], axis=0)
        back = jnp.concatenate([edge, product[PAIR:], edge], axis=0)
        main = main + forth[tap * DILATION : tap * DILATION + rows]
        mirror = mirror + back[(2 - tap) * DILATION : (2 - tap) * DILATION + rows]
    pre[0, 0:rows] = main
    pre[1, 0:rows] = mirror
    pre[:, rows:ROWS] = jnp.zeros((2, ROWS - rows, HID), F32)
    copy = pltpu.make_async_copy(pre, out, sem)
    copy.start()
    turn(normed, channels(), 1 - core(), others)
    turn(normed, channels(), core(), mine)
    copy.wait()


def slope_kernel(s0, s1, s3, s2, table, wp, taps, inner, pre, gp, bin_grad, wide, spread):
    reverse = reverser()
    pair = seat() // 2
    odd = seat() % 2
    row = lax.broadcasted_iota(jnp.int32, (128, EXONS), 0)
    owner = ((row >> 4) & 1) * 4 + ((row >> 5) ^ (seat() & 3))
    genes = jnp.where((row & 15) < 8, owner * 8 + (row & 7), -1)
    table = table()[...]
    inside = pool_inside(table, pair * PAIR - DILATION, ROWS)
    counts = dot(inside, pool_member(table, genes), 1, 1).astype(BF)
    for apart, piece in enumerate((s0, s1, s2, s3)):
        spread[apart] = piece()[...]
    wide[...] = dot(counts, spread[...].reshape(128, C), 1, 0)
    covered = wide[...].astype(BF)
    own = pl.multiple_of(odd * BINS, BINS)
    bin_grad[...] = wide[pl.ds(own, BINS + 8)][DILATION : DILATION + BINS].astype(BF)
    both = jnp.concatenate([covered, flip_channels(covered, reverse)], axis=0)
    grad_act = dot(both, wp()[...], 1, 0)

    before = jnp.maximum(2 * pair - 1, 0)
    beyond = jnp.minimum(2 * pair + 2, 7)
    left = spread[(before ^ seat()) & 3, before // 4][8 : 8 + HALO].astype(F32)
    right = spread[(beyond ^ seat()) & 3, beyond // 4][8 : 8 + HALO].astype(F32)
    halo = jnp.concatenate([jnp.where(pair > 0, left, 0.0), jnp.where(pair < 3, right, 0.0)], axis=0)
    halo = normalized(halo)
    halo = jnp.concatenate([halo, flip_channels(halo, reverse)], axis=0)
    rest = jnp.zeros((DILATION, HID), F32)
    sums = [jnp.zeros((HALO, HID), F32) for _ in range(4)]
    for tap in range(3):
        product = dot(halo, taps[tap]()[...], 1, 0)
        for branch in range(2):
            left = product[2 * HALO * branch : 2 * HALO * branch + HALO]
            right = product[2 * HALO * branch + HALO : 2 * HALO * branch + 2 * HALO]
            shift = tap if branch == 0 else 2 - tap
            if shift == 0:
                sums[2 * branch] += left
            elif shift == 1:
                sums[2 * branch] += jnp.concatenate([left[DILATION:], rest], axis=0)
                sums[2 * branch + 1] += jnp.concatenate([rest, right[:DILATION]], axis=0)
            else:
                sums[2 * branch + 1] += right
    pre[...] = inner()[...]
    for branch in range(2):
        pre[branch, 0:HALO] = pre[branch, 0:HALO] + sums[2 * branch]
        pre[branch, PAIR : PAIR + HALO] = pre[branch, PAIR : PAIR + HALO] + sums[2 * branch + 1]
    gp[0] = (grad_act[0:ROWS] * gelu_slope(pre[0])).astype(BF)
    gp[1] = (grad_act[ROWS:] * gelu_slope(pre[1])).astype(BF)


def weight_kernel(turned, turned_other, own, other, after, out, done):
    del after
    done[...] = jnp.zeros((8, 128), F32)
    wide = [[ref()[branch].astype(F32) for branch in range(2)] for ref in (own, other)]
    for tap in range(3):
        total = jnp.zeros((QUARTER, HID), F32)
        for ref, grads in zip((turned, turned_other), wide):
            main = grads[0][(2 - tap) * DILATION : (2 - tap) * DILATION + PAIR]
            mirror = grads[1][tap * DILATION : tap * DILATION + PAIR]
            total = total + dot(ref()[...], jnp.concatenate([main, mirror], axis=0).astype(BF), 1, 0)
        out[:, tap] = (total * (1.0 / 32)).astype(BF).reshape(8, 48, HID)


def plane_sum_kernel(terms, out):
    total = terms[0].astype(F32)
    for k in range(1, 8):
        total = total + terms[k].astype(F32)
    for k in range(8):
        out[k] = total[:, 6 * k : 6 * k + 6].astype(BF)


def column_sum_kernel(terms, out):
    total = terms[0].astype(F32)
    for k in range(1, 8):
        total = total + terms[k].astype(F32)
    for tap in range(3):
        out[:, tap] = total[tap]


def output_kernel(tok, partner, pre, wp, table, give, keep, done):
    done[...] = jnp.zeros((8, 128), F32)
    odd = seat() % 2
    pre = pre()
    acts = [gelu_value(pre[branch][DILATION : DILATION + PAIR]).astype(BF) for branch in range(2)]
    outs = dot(jnp.concatenate(acts, axis=0), wp()[...], 1, 1).astype(BF)
    mirror = flip_channels(outs[PAIR:], reverser())
    low, high = in_order(odd, tok()[...].astype(F32), partner()[...].astype(F32))
    block = jnp.concatenate([low, high], axis=0)
    block = (block + outs[0:PAIR].astype(F32) + mirror.astype(F32)).astype(BF)
    table = table()[...]
    inside = pool_inside(table, (seat() // 2) * PAIR, PAIR)
    row = lax.broadcasted_iota(jnp.int32, (GENES // 2, table.shape[1]), 0)
    genes = (row >> 3) * 16 + odd * 8 + (row & 7)
    counts = dot(pool_member(table, genes), inside, 1, 1).astype(BF)
    partial = dot(counts, block, 1, 0)
    half = (seat() // 2) % 2
    low = jnp.concatenate([partial[0:8], partial[16:24]], axis=0)
    high = jnp.concatenate([partial[8:16], partial[24:32]], axis=0)
    give[...] = jnp.where(half == 0, high, low).astype(BF)
    keep[...] = jnp.where(half == 0, low, high)


def input_kernel(tok, gp, bin_grad, taps, after, out):
    del after
    odd = seat() % 2
    wide = tok()[...].astype(F32)
    scale = row_scale(wide)
    unit = wide * scale
    reverse = reverser()
    mirror_unit = flip_channels(tok()[...], reverse).astype(F32) * scale
    start = pl.multiple_of(odd * BINS, BINS)
    shifted = [gp()[branch, pl.ds(start, BINS + 16)].astype(F32) for branch in range(2)]
    total = jnp.zeros((2 * BINS, C), F32)
    for tap in range(3):
        main = shifted[0][(2 - tap) * DILATION : (2 - tap) * DILATION + BINS]
        mirror = shifted[1][tap * DILATION : tap * DILATION + BINS]
        total = total + dot(jnp.concatenate([main, mirror], axis=0).astype(BF), taps[tap]()[...], 1, 1)
    parts = []
    for grad, part in ((total[0:BINS], unit), (total[BINS:], mirror_unit)):
        centred = grad - part * jnp.mean(grad * part, axis=1, keepdims=True)
        parts.append((centred * scale).astype(BF))
    mirror = flip_channels(parts[1], reverse)
    out[...] = (bin_grad()[...].astype(F32) + parts[0].astype(F32) + mirror.astype(F32)).astype(BF)


def shape(dims, kind):
    return jax.ShapeDtypeStruct(dims, kind)


class Fetched:
    def __init__(self, source, buffer, sem):
        self.copy = pltpu.make_async_copy(source, buffer, sem)
        self.buffer = buffer
        self.waits = True
        self.copy.start()

    def __call__(self):
        if self.waits:
            self.copy.wait()
            self.waits = False
        return self.buffer


def call(kernel, out_shape, *args, order=(), large=(), far=(), pinned=False, scratch=(), work=1):
    outs = len(out_shape) if isinstance(out_shape, tuple) else 1
    places = [pl.BlockSpec(memory_space=pltpu.HBM if at in far else None) for at in range(outs)]
    count = len(args)
    if pinned:
        specs = [pl.BlockSpec(memory_space=pltpu.VMEM)] * count
        body, buffers = kernel, []
    else:
        args = list(args)
        specs = [pl.BlockSpec(memory_space=pl.ANY)] * count
        for at in large:
            specs[at] = pl.BlockSpec(memory_space=pltpu.HBM)
            args[at] = pltpu.with_memory_space_constraint(args[at], pltpu.HBM)
        fetched = [at for at in range(count) if at not in order]
        tapped = [at for at in fetched if args[at].shape == (3, C, HID)]
        buffers = [pltpu.VMEM(args[at].shape, args[at].dtype) for at in fetched]
        buffers.append(pltpu.SemaphoreType.DMA((len(fetched) + 2,)))

        def body(*refs):
            values = list(refs[:count])
            held = refs[count + outs : count + outs + len(fetched)]
            sems = refs[count + outs + len(fetched)]
            for k, at in enumerate(fetched):
                if at in tapped:
                    lanes = [k, len(fetched), len(fetched) + 1]
                    values[at] = [
                        Fetched(refs[at].at[tap], held[k].at[tap], sems.at[lanes[tap]])
                        for tap in range(3)
                    ]
                else:
                    values[at] = Fetched(refs[at], held[k], sems.at[k])
            kernel(*values, *refs[count : count + outs], *refs[count + outs + len(fetched) + 1 :])

    return pl.pallas_call(
        body,
        out_shape=out_shape,
        in_specs=specs,
        out_specs=tuple(places) if isinstance(out_shape, tuple) else places[0],
        scratch_shapes=buffers + list(scratch),
        cost_estimate=pl.CostEstimate(flops=int(work * 1e9), transcendentals=0, bytes_accessed=0),
        compiler_params=pltpu.CompilerParams(vmem_limit_bytes=VMEM_LIMIT),
    )(*args)


def pack(tok, grads):
    return pl.pallas_call(
        pack_kernel,
        grid=(1,),
        out_shape=shape((16, C), BF),
        in_specs=[
            pl.BlockSpec((HALO, C), lambda i: (0, 0)),
            pl.BlockSpec((HALO, C), lambda i: (BINS // HALO - 1, 0)),
            pl.BlockSpec((8, C), lambda i: (0, 0)),
        ],
        out_specs=pl.BlockSpec((16, C), lambda i: (0, 0)),
    )(tok, tok, grads)


DONE = jax.ShapeDtypeStruct((8, 128), F32)


def scatter_genes(give, keep):
    values = keep + lax.ppermute(give, "seq", [(s, s ^ 2) for s in range(8)]).astype(F32)
    upper = seat() // 4
    keep = jnp.where(upper == 0, values[:8], values[8:])
    give = jnp.where(upper == 0, values[8:], values[:8]).astype(BF)
    return keep + lax.ppermute(give, "seq", [(s, s ^ 4) for s in range(8)]).astype(F32)


def local(tokens, w_conv, w_point, exon_table, gene_grads):
    tok = tokens[0]
    table = exon_table[0]
    taps = jnp.transpose(w_conv, (1, 0, 2))
    pair_rows = shape((2, ROWS, HID), F32)

    partner = lax.ppermute(tok, "seq", SEQ_PAIRS)
    mine = pack(tok, gene_grads[0])
    across = lax.ppermute(mine, "seq", [(s, s ^ 4) for s in range(8)])
    both, ready = call(
        both_kernel, (shape((2, 16, C), BF), DONE), mine, across, pinned=True, work=SUM_WORK
    )
    spread = [both]
    for apart in (1, 3, 2):
        spread.append(lax.ppermute(both, "seq", [(s, s ^ apart) for s in range(8)]))

    quarter = shape((QUARTER, 2 * PAIR), BF)
    inner, turned, lent = call(
        forward_kernel,
        (pair_rows, quarter, quarter),
        tok,
        partner,
        taps,
        jnp.asarray(CHANNELS),
        ready,
        large=(0, 2),
        order=(4,),
        far=(0,),
        scratch=[pltpu.VMEM((2, ROWS, HID), F32), pltpu.SemaphoreType.DMA],
        work=FORWARD_WORK,
    )
    turned_other = lax.ppermute(lent, "batch", CORE_PAIRS)
    pre, gp, bin_grad = call(
        slope_kernel,
        (pair_rows, shape((2, ROWS, HID), BF), shape((BINS, C), BF)),
        *spread,
        table,
        w_point,
        taps,
        inner,
        large=(5, 6),
        work=SLOPE_WORK,
        scratch=[pltpu.VMEM((ROWS, C), F32), pltpu.VMEM((4, 2, 16, C), BF)],
    )
    gp_other = lax.ppermute(gp, "batch", CORE_PAIRS)
    give, keep, output_done = call(
        output_kernel,
        (shape((GENES // 4, C), BF), shape((GENES // 4, C), F32), DONE),
        tok,
        partner,
        pre,
        w_point,
        table,
        large=(0, 3),
        work=OUTPUT_WORK,
    )
    pooled = scatter_genes(give, keep)
    terms, terms_done = call(
        weight_kernel,
        (shape((8, 3, 48, HID), BF), DONE),
        turned,
        turned_other,
        gp,
        gp_other,
        output_done,
        order=(4,),
    )
    grad_input = call(
        input_kernel,
        shape((BINS, C), BF),
        tok,
        gp,
        bin_grad,
        taps,
        terms_done,
        large=(0, 3),
        order=(4,),
        work=INPUT_WORK,
    )
    terms = lax.all_to_all(terms, ("batch", "seq"), 0, 0, tiled=True, axis_index_groups=PLANES)
    terms = call(plane_sum_kernel, shape((8, 3, 6, HID), BF), terms, pinned=True, work=SUM_WORK)
    terms = lax.all_to_all(terms, ("batch", "seq"), 0, 0, tiled=True, axis_index_groups=COLUMNS)
    total = call(column_sum_kernel, shape((6, 3, HID), F32), terms, pinned=True, work=SUM_WORK)
    return (pooled[None], grad_input[None], total)


def solution(mesh):
    placed = (P("batch", "seq", None), P(), P(), P("batch", None, None), P("batch", "seq", None))
    return jax.shard_map(
        local,
        mesh=mesh,
        in_specs=placed,
        out_specs=(
            P("batch", "seq", None),
            P("batch", "seq", None),
            P(("batch", "seq"), None, None),
        ),
        check_vma=False,
    )
```

```python
import jax
import jax.numpy as jnp
import numpy as np
from jax import lax
from jax.experimental import pallas as pl
from jax.experimental.pallas import tpu as pltpu
from jax.sharding import PartitionSpec as P

DILATION = 4
GENES = 64
EXONS = 256
EPSILON = 1e-06
INVERSE_ROOT_TWO = 0.7071067811865476
INVERSE_ROOT_TAU = 0.3989422804014327

BINS = 128
PAIR = 2 * BINS
HALO = 8
ROWS = PAIR + 2 * HALO
C = 1536
HID = 384
QUARTER = C // 4
FLIP = 256
BF = jnp.bfloat16
F32 = jnp.float32
VMEM_LIMIT = 28 * 1024 * 1024

TURN_WORK = 1
GRADIENT_WORK = 3
OUTPUT_WORK = 0.3
INPUT_WORK = 0.9
SUM_WORK = 1
CORE_PAIRS = [(b, b ^ 1) for b in range(32)]
SEQ_PAIRS = [(s, s ^ 1) for s in range(8)]


def linear(z_hi, x, z_lo, y, core):
    return ((z_lo * 4 + y) * 2 + core) * 8 + z_hi * 4 + x


PLANES = [
    [linear(zh, 2 * half + odd, zl, y, c) for y in range(4) for half in range(2)]
    for odd in range(2)
    for zh in range(2)
    for zl in range(4)
    for c in range(2)
]
COLUMNS = [
    [linear(zh, x, zl, y, c) for zh in range(2) for zl in range(4)]
    for x in range(4)
    for y in range(4)
    for c in range(2)
]
CHANNELS = np.array(
    [
        6 * linear(zh, 2 * half, zl, y, 0) + k
        for y in range(4)
        for half in range(2)
        for zh in range(2)
        for zl in range(4)
        for k in range(6)
    ],
    dtype=np.int32,
).reshape(QUARTER, 1)


def dot(a, b, da, db):
    return lax.dot_general(a, b, (((da,), (db,)), ((), ())), preferred_element_type=F32)


def cumulative(values):
    return 0.5 * (1.0 + lax.erf(values * INVERSE_ROOT_TWO))


def gelu_value(values):
    return values * cumulative(values)


def gelu_slope(values):
    return cumulative(values) + values * jnp.exp(-0.5 * values * values) * INVERSE_ROOT_TAU


def reverser():
    rows = lax.broadcasted_iota(jnp.int32, (FLIP, FLIP), 0)
    cols = lax.broadcasted_iota(jnp.int32, (FLIP, FLIP), 1)
    return jnp.where(rows + cols == FLIP - 1, 1.0, 0.0).astype(BF)


def flip_channels(values, turn):
    parts = []
    for k in reversed(range(C // FLIP)):
        parts.append(dot(values[:, k * FLIP : (k + 1) * FLIP], turn, 1, 0).astype(BF))
    return jnp.concatenate(parts, axis=1)


def row_scale(wide):
    return lax.rsqrt(jnp.mean(wide * wide, axis=1, keepdims=True) + EPSILON)


def pool_inside(table, first_bin, rows):
    positions = first_bin + lax.broadcasted_iota(jnp.int32, (rows, table.shape[1]), 0)
    inside = (positions >= table[1:2, :]) & (positions < table[2:3, :])
    return jnp.where(inside, 1.0, 0.0).astype(BF)


def pool_member(table, genes):
    return jnp.where(genes == table[0:1, :], 1.0, 0.0).astype(BF)


def seat():
    return lax.axis_index("seq").astype(jnp.int32)


def core():
    return lax.axis_index("batch").astype(jnp.int32) % 2


def pack_kernel(head, tail, grads, out):
    edge = jnp.where(seat() % 2 == 1, tail[...].astype(F32), head[...].astype(F32))
    out[...] = jnp.concatenate([grads[...].astype(F32), edge], axis=0).astype(BF)


def both_kernel(mine, across, out, done):
    upper = seat() // 4
    low, high = in_order(upper, mine[...].astype(F32), across[...].astype(F32))
    out[0] = low.astype(BF)
    out[1] = high.astype(BF)
    done[...] = jnp.zeros((8, 128), F32)


def in_order(odd, own, partner):
    return jnp.where(odd == 0, own, partner), jnp.where(odd == 0, partner, own)


def normalized(wide):
    return (wide * row_scale(wide)).astype(BF)


def turn(normed, channels, core_index, out):
    wanted = channels[...] + 6 * (seat() % 2) + 48 * core_index
    main = jnp.zeros((QUARTER, PAIR), F32)
    mirror = jnp.zeros((QUARTER, PAIR), F32)
    for k in range(C // FLIP):
        lane = k * FLIP + lax.broadcasted_iota(jnp.int32, (QUARTER, FLIP), 1)
        piece = normed[:, k * FLIP : (k + 1) * FLIP]
        pick = jnp.where(lane == wanted, 1.0, 0.0).astype(BF)
        main = main + dot(pick, piece, 1, 1)
        pick = jnp.where(C - 1 - lane == wanted, 1.0, 0.0).astype(BF)
        mirror = mirror + dot(pick, piece, 1, 1)
    out[:, 0:PAIR] = main.astype(BF)
    out[:, PAIR:] = mirror.astype(BF)


def turn_kernel(own, partner, channels, after, out, others, done, mine, sem):
    del after
    done[...] = jnp.zeros((8, 128), F32)
    low, high = in_order(seat() % 2, own()[...].astype(F32), partner()[...].astype(F32))
    normed = normalized(jnp.concatenate([low, high], axis=0))
    turn(normed, channels(), core(), mine)
    copy = pltpu.make_async_copy(mine, out, sem)
    copy.start()
    turn(normed, channels(), 1 - core(), others)
    copy.wait()


def gradient_kernel(
    tok, partner, s0, s1, s3, s2, table, taps, wp, after, pre, gp, bin_grad, wide, spread
):
    del after
    reverse = reverser()
    pair = seat() // 2
    odd = seat() % 2
    low, high = in_order(odd, tok()[...].astype(F32), partner()[...].astype(F32))
    for apart, piece in enumerate((s0, s1, s2, s3)):
        spread[apart] = piece()[...]
    before = jnp.maximum(2 * pair - 1, 0)
    beyond = jnp.minimum(2 * pair + 2, 7)
    left = spread[(before ^ seat()) & 3, before // 4][8 : 8 + HALO].astype(F32)
    right = spread[(beyond ^ seat()) & 3, beyond // 4][8 : 8 + HALO].astype(F32)
    left = jnp.where(pair > 0, left, 0.0)
    right = jnp.where(pair < 3, right, 0.0)
    normed = normalized(jnp.concatenate([left, low, high, right], axis=0))
    both = jnp.concatenate([normed, flip_channels(normed, reverse)], axis=0)
    rows = PAIR + 2 * DILATION
    main = jnp.zeros((rows, HID), F32)
    mirror = jnp.zeros((rows, HID), F32)
    for tap in range(3):
        product = dot(both, taps[tap]()[...], 1, 0)
        main = main + product[tap * DILATION : tap * DILATION + rows]
        at = ROWS + (2 - tap) * DILATION
        mirror = mirror + product[at : at + rows]
    pre[0, 0:rows] = main
    pre[1, 0:rows] = mirror
    pre[:, rows:ROWS] = jnp.zeros((2, ROWS - rows, HID), F32)

    row = lax.broadcasted_iota(jnp.int32, (128, EXONS), 0)
    owner = ((row >> 4) & 1) * 4 + ((row >> 5) ^ (seat() & 3))
    genes = jnp.where((row & 15) < 8, owner * 8 + (row & 7), -1)
    table = table()[...]
    inside = pool_inside(table, pair * PAIR - DILATION, ROWS)
    counts = dot(inside, pool_member(table, genes), 1, 1).astype(BF)
    wide[...] = dot(counts, spread[...].reshape(128, C), 1, 0)
    covered = wide[...].astype(BF)
    own = pl.multiple_of(odd * BINS, BINS)
    bin_grad[...] = wide[pl.ds(own, BINS + 8)][DILATION : DILATION + BINS].astype(BF)
    both = jnp.concatenate([covered, flip_channels(covered, reverse)], axis=0)
    grad_act = dot(both, wp()[...], 1, 0)
    gp[0] = (grad_act[0:ROWS] * gelu_slope(pre[0])).astype(BF)
    gp[1] = (grad_act[ROWS:] * gelu_slope(pre[1])).astype(BF)


def weight_kernel(turned, turned_other, own, other, after, out, done):
    del after
    done[...] = jnp.zeros((8, 128), F32)
    wide = [[ref()[branch].astype(F32) for branch in range(2)] for ref in (own, other)]
    for tap in range(3):
        total = jnp.zeros((QUARTER, HID), F32)
        for ref, grads in zip((turned, turned_other), wide):
            main = grads[0][(2 - tap) * DILATION : (2 - tap) * DILATION + PAIR]
            mirror = grads[1][tap * DILATION : tap * DILATION + PAIR]
            total = total + dot(ref()[...], jnp.concatenate([main, mirror], axis=0).astype(BF), 1, 0)
        out[:, tap] = (total * (1.0 / 32)).astype(BF).reshape(8, 48, HID)


def plane_sum_kernel(terms, after, out):
    del after
    total = terms[0].astype(F32)
    for k in range(1, 8):
        total = total + terms[k].astype(F32)
    for k in range(8):
        out[k] = total[:, 6 * k : 6 * k + 6].astype(BF)


def column_sum_kernel(terms, out):
    total = terms[0].astype(F32)
    for k in range(1, 8):
        total = total + terms[k].astype(F32)
    for tap in range(3):
        out[:, tap] = total[tap]


def output_kernel(tok, partner, pre, wp, table, give, keep, done):
    done[...] = jnp.zeros((8, 128), F32)
    odd = seat() % 2
    pre = pre()
    acts = [gelu_value(pre[branch][DILATION : DILATION + PAIR]).astype(BF) for branch in range(2)]
    outs = dot(jnp.concatenate(acts, axis=0), wp()[...], 1, 1).astype(BF)
    mirror = flip_channels(outs[PAIR:], reverser())
    low, high = in_order(odd, tok()[...].astype(F32), partner()[...].astype(F32))
    block = jnp.concatenate([low, high], axis=0)
    block = (block + outs[0:PAIR].astype(F32) + mirror.astype(F32)).astype(BF)
    table = table()[...]
    inside = pool_inside(table, (seat() // 2) * PAIR, PAIR)
    row = lax.broadcasted_iota(jnp.int32, (GENES // 2, table.shape[1]), 0)
    genes = (row >> 3) * 16 + odd * 8 + (row & 7)
    counts = dot(pool_member(table, genes), inside, 1, 1).astype(BF)
    partial = dot(counts, block, 1, 0)
    half = (seat() // 2) % 2
    low = jnp.concatenate([partial[0:8], partial[16:24]], axis=0)
    high = jnp.concatenate([partial[8:16], partial[24:32]], axis=0)
    give[...] = jnp.where(half == 0, high, low).astype(BF)
    keep[...] = jnp.where(half == 0, low, high)


def input_kernel(tok, gp, bin_grad, taps, after, out, done):
    del after
    done[...] = jnp.zeros((8, 128), F32)
    odd = seat() % 2
    wide = tok()[...].astype(F32)
    scale = row_scale(wide)
    unit = wide * scale
    reverse = reverser()
    mirror_unit = flip_channels(tok()[...], reverse).astype(F32) * scale
    start = pl.multiple_of(odd * BINS, BINS)
    shifted = [gp()[branch, pl.ds(start, BINS + 16)].astype(F32) for branch in range(2)]
    total = jnp.zeros((2 * BINS, C), F32)
    for tap in range(3):
        main = shifted[0][(2 - tap) * DILATION : (2 - tap) * DILATION + BINS]
        mirror = shifted[1][tap * DILATION : tap * DILATION + BINS]
        total = total + dot(jnp.concatenate([main, mirror], axis=0).astype(BF), taps[tap]()[...], 1, 1)
    parts = []
    for grad, part in ((total[0:BINS], unit), (total[BINS:], mirror_unit)):
        centred = grad - part * jnp.mean(grad * part, axis=1, keepdims=True)
        parts.append((centred * scale).astype(BF))
    mirror = flip_channels(parts[1], reverse)
    out[...] = (bin_grad()[...].astype(F32) + parts[0].astype(F32) + mirror.astype(F32)).astype(BF)


def shape(dims, kind):
    return jax.ShapeDtypeStruct(dims, kind)


class Fetched:
    def __init__(self, source, buffer, sem):
        self.copy = pltpu.make_async_copy(source, buffer, sem)
        self.buffer = buffer
        self.waits = True
        self.copy.start()

    def __call__(self):
        if self.waits:
            self.copy.wait()
            self.waits = False
        return self.buffer


def call(kernel, out_shape, *args, order=(), large=(), far=(), pinned=False, scratch=(), work=1):
    outs = len(out_shape) if isinstance(out_shape, tuple) else 1
    places = [pl.BlockSpec(memory_space=pltpu.HBM if at in far else None) for at in range(outs)]
    count = len(args)
    if pinned:
        specs = [pl.BlockSpec(memory_space=pltpu.VMEM)] * count
        body, buffers = kernel, []
    else:
        args = list(args)
        specs = [pl.BlockSpec(memory_space=pl.ANY)] * count
        for at in large:
            specs[at] = pl.BlockSpec(memory_space=pltpu.HBM)
            args[at] = pltpu.with_memory_space_constraint(args[at], pltpu.HBM)
        fetched = [at for at in range(count) if at not in order]
        tapped = [at for at in fetched if args[at].shape == (3, C, HID)]
        buffers = [pltpu.VMEM(args[at].shape, args[at].dtype) for at in fetched]
        buffers.append(pltpu.SemaphoreType.DMA((len(fetched) + 2,)))

        def body(*refs):
            values = list(refs[:count])
            held = refs[count + outs : count + outs + len(fetched)]
            sems = refs[count + outs + len(fetched)]
            for k, at in enumerate(fetched):
                if at in tapped:
                    lanes = [k, len(fetched), len(fetched) + 1]
                    values[at] = [
                        Fetched(refs[at].at[tap], held[k].at[tap], sems.at[lanes[tap]])
                        for tap in range(3)
                    ]
                else:
                    values[at] = Fetched(refs[at], held[k], sems.at[k])
            kernel(*values, *refs[count : count + outs], *refs[count + outs + len(fetched) + 1 :])

    return pl.pallas_call(
        body,
        out_shape=out_shape,
        in_specs=specs,
        out_specs=tuple(places) if isinstance(out_shape, tuple) else places[0],
        scratch_shapes=buffers + list(scratch),
        cost_estimate=pl.CostEstimate(flops=int(work * 1e9), transcendentals=0, bytes_accessed=0),
        compiler_params=pltpu.CompilerParams(vmem_limit_bytes=VMEM_LIMIT),
    )(*args)


def pack(tok, grads):
    return pl.pallas_call(
        pack_kernel,
        grid=(1,),
        out_shape=shape((16, C), BF),
        in_specs=[
            pl.BlockSpec((HALO, C), lambda i: (0, 0)),
            pl.BlockSpec((HALO, C), lambda i: (BINS // HALO - 1, 0)),
            pl.BlockSpec((8, C), lambda i: (0, 0)),
        ],
        out_specs=pl.BlockSpec((16, C), lambda i: (0, 0)),
    )(tok, tok, grads)


DONE = jax.ShapeDtypeStruct((8, 128), F32)


def scatter_genes(give, keep):
    values = keep + lax.ppermute(give, "seq", [(s, s ^ 2) for s in range(8)]).astype(F32)
    upper = seat() // 4
    keep = jnp.where(upper == 0, values[:8], values[8:])
    give = jnp.where(upper == 0, values[8:], values[:8]).astype(BF)
    return keep + lax.ppermute(give, "seq", [(s, s ^ 4) for s in range(8)]).astype(F32)


def local(tokens, w_conv, w_point, exon_table, gene_grads):
    tok = tokens[0]
    table = exon_table[0]
    taps = jnp.transpose(w_conv, (1, 0, 2))
    pair_rows = shape((2, ROWS, HID), F32)

    partner = lax.ppermute(tok, "seq", SEQ_PAIRS)
    mine = pack(tok, gene_grads[0])
    across = lax.ppermute(mine, "seq", [(s, s ^ 4) for s in range(8)])
    both, ready = call(
        both_kernel, (shape((2, 16, C), BF), DONE), mine, across, pinned=True, work=SUM_WORK
    )
    spread = [both]
    for apart in (1, 3, 2):
        spread.append(lax.ppermute(both, "seq", [(s, s ^ apart) for s in range(8)]))

    quarter = shape((QUARTER, 2 * PAIR), BF)
    turned, lent, turn_done = call(
        turn_kernel,
        (quarter, quarter, DONE),
        tok,
        partner,
        jnp.asarray(CHANNELS),
        ready,
        large=(0,),
        order=(3,),
        far=(0,),
        scratch=[pltpu.VMEM((QUARTER, 2 * PAIR), BF), pltpu.SemaphoreType.DMA],
        work=TURN_WORK,
    )
    turned_other = lax.ppermute(lent, "batch", CORE_PAIRS)
    pre, gp, bin_grad = call(
        gradient_kernel,
        (pair_rows, shape((2, ROWS, HID), BF), shape((BINS, C), BF)),
        tok,
        partner,
        *spread,
        table,
        taps,
        w_point,
        turn_done,
        large=(0, 7, 8),
        order=(9,),
        work=GRADIENT_WORK,
        scratch=[pltpu.VMEM((ROWS, C), F32), pltpu.VMEM((4, 2, 16, C), BF)],
    )
    gp_other = lax.ppermute(gp, "batch", CORE_PAIRS)
    give, keep, output_done = call(
        output_kernel,
        (shape((GENES // 4, C), BF), shape((GENES // 4, C), F32), DONE),
        tok,
        partner,
        pre,
        w_point,
        table,
        large=(0, 3),
        work=OUTPUT_WORK,
    )
    pooled = scatter_genes(give, keep)
    terms, terms_done = call(
        weight_kernel,
        (shape((8, 3, 48, HID), BF), DONE),
        turned,
        turned_other,
        gp,
        gp_other,
        output_done,
        large=(0,),
        order=(4,),
    )
    grad_input, input_done = call(
        input_kernel,
        (shape((BINS, C), BF), DONE),
        tok,
        gp,
        bin_grad,
        taps,
        terms_done,
        large=(0, 3),
        order=(4,),
        work=INPUT_WORK,
    )
    terms = lax.all_to_all(terms, ("batch", "seq"), 0, 0, tiled=True, axis_index_groups=PLANES)
    terms = call(
        plane_sum_kernel, shape((8, 3, 6, HID), BF), terms, input_done, pinned=True, work=SUM_WORK
    )
    terms = lax.all_to_all(terms, ("batch", "seq"), 0, 0, tiled=True, axis_index_groups=COLUMNS)
    total = call(column_sum_kernel, shape((6, 3, HID), F32), terms, pinned=True, work=SUM_WORK)
    return (pooled[None], grad_input[None], total)


def solution(mesh):
    placed = (P("batch", "seq", None), P(), P(), P("batch", None, None), P("batch", "seq", None))
    return jax.shard_map(
        local,
        mesh=mesh,
        in_specs=placed,
        out_specs=(
            P("batch", "seq", None),
            P("batch", "seq", None),
            P(("batch", "seq"), None, None),
        ),
        check_vma=False,
    )
```

```python
import jax
import jax.numpy as jnp
import numpy as np
from jax import lax
from jax.experimental import pallas as pl
from jax.experimental.pallas import tpu as pltpu
from jax.sharding import PartitionSpec as P

DILATION = 4
GENES = 64
EXONS = 256
EPSILON = 1e-06
INVERSE_ROOT_TWO = 0.7071067811865476
INVERSE_ROOT_TAU = 0.3989422804014327

BINS = 128
PAIR = 2 * BINS
HALO = 8
ROWS = PAIR + 2 * HALO
C = 1536
HID = 384
QUARTER = C // 4
FLIP = 256
BF = jnp.bfloat16
F32 = jnp.float32
VMEM_LIMIT = 28 * 1024 * 1024

FORWARD_WORK = 0.5
SLOPE_WORK = 2
OUTPUT_WORK = 0.3
INPUT_WORK = 0.9
SUM_WORK = 1
CORE_PAIRS = [(b, b ^ 1) for b in range(32)]
SEQ_PAIRS = [(s, s ^ 1) for s in range(8)]


def linear(z_hi, x, z_lo, y, core):
    return ((z_lo * 4 + y) * 2 + core) * 8 + z_hi * 4 + x


PLANES = [
    [linear(zh, 2 * half + odd, zl, y, c) for y in range(4) for half in range(2)]
    for odd in range(2)
    for zh in range(2)
    for zl in range(4)
    for c in range(2)
]
COLUMNS = [
    [linear(zh, x, zl, y, c) for zh in range(2) for zl in range(4)]
    for x in range(4)
    for y in range(4)
    for c in range(2)
]
CHANNELS = np.array(
    [
        6 * linear(zh, 2 * half, zl, y, 0) + k
        for y in range(4)
        for half in range(2)
        for zh in range(2)
        for zl in range(4)
        for k in range(6)
    ],
    dtype=np.int32,
).reshape(QUARTER, 1)


def dot(a, b, da, db):
    return lax.dot_general(a, b, (((da,), (db,)), ((), ())), preferred_element_type=F32)


def cumulative(values):
    return 0.5 * (1.0 + lax.erf(values * INVERSE_ROOT_TWO))


def gelu_value(values):
    return values * cumulative(values)


def gelu_slope(values):
    return cumulative(values) + values * jnp.exp(-0.5 * values * values) * INVERSE_ROOT_TAU


def reverser():
    rows = lax.broadcasted_iota(jnp.int32, (FLIP, FLIP), 0)
    cols = lax.broadcasted_iota(jnp.int32, (FLIP, FLIP), 1)
    return jnp.where(rows + cols == FLIP - 1, 1.0, 0.0).astype(BF)


def flip_channels(values, turn):
    parts = []
    for k in reversed(range(C // FLIP)):
        parts.append(dot(values[:, k * FLIP : (k + 1) * FLIP], turn, 1, 0).astype(BF))
    return jnp.concatenate(parts, axis=1)


def row_scale(wide):
    return lax.rsqrt(jnp.mean(wide * wide, axis=1, keepdims=True) + EPSILON)


def pool_inside(table, first_bin, rows):
    positions = first_bin + lax.broadcasted_iota(jnp.int32, (rows, table.shape[1]), 0)
    inside = (positions >= table[1:2, :]) & (positions < table[2:3, :])
    return jnp.where(inside, 1.0, 0.0).astype(BF)


def pool_member(table, genes):
    return jnp.where(genes == table[0:1, :], 1.0, 0.0).astype(BF)


def seat():
    return lax.axis_index("seq").astype(jnp.int32)


def core():
    return lax.axis_index("batch").astype(jnp.int32) % 2


def pack_kernel(head, tail, grads, out):
    edge = jnp.where(seat() % 2 == 1, tail[...].astype(F32), head[...].astype(F32))
    out[...] = jnp.concatenate([grads[...].astype(F32), edge], axis=0).astype(BF)


def both_kernel(mine, across, out, done):
    upper = seat() // 4
    low, high = in_order(upper, mine()[...].astype(F32), across()[...].astype(F32))
    out[0] = low.astype(BF)
    out[1] = high.astype(BF)
    done[...] = jnp.zeros((8, 128), F32)


def in_order(odd, own, partner):
    return jnp.where(odd == 0, own, partner), jnp.where(odd == 0, partner, own)


def normalized(wide):
    return (wide * row_scale(wide)).astype(BF)


def turn(normed, channels, core_index, out):
    wanted = channels[...] + 6 * (seat() % 2) + 48 * core_index
    main = jnp.zeros((QUARTER, PAIR), F32)
    mirror = jnp.zeros((QUARTER, PAIR), F32)
    for k in range(C // FLIP):
        lane = k * FLIP + lax.broadcasted_iota(jnp.int32, (QUARTER, FLIP), 1)
        piece = normed[:, k * FLIP : (k + 1) * FLIP]
        pick = jnp.where(lane == wanted, 1.0, 0.0).astype(BF)
        main = main + dot(pick, piece, 1, 1)
        pick = jnp.where(C - 1 - lane == wanted, 1.0, 0.0).astype(BF)
        mirror = mirror + dot(pick, piece, 1, 1)
    out[:, 0:PAIR] = main.astype(BF)
    out[:, PAIR:] = mirror.astype(BF)


def forward_kernel(tok, partner, taps, channels, after, out, mine, others, pre, sem):
    del after
    low, high = in_order(seat() % 2, tok()[...].astype(F32), partner()[...].astype(F32))
    normed = normalized(jnp.concatenate([low, high], axis=0))
    both = jnp.concatenate([normed, flip_channels(normed, reverser())], axis=0)
    rows = PAIR + 2 * DILATION
    edge = jnp.zeros((HALO, HID), F32)
    main = jnp.zeros((rows, HID), F32)
    mirror = jnp.zeros((rows, HID), F32)
    for tap in range(3):
        product = dot(both, taps[tap]()[...], 1, 0)
        forth = jnp.concatenate([edge, product[0:PAIR], edge], axis=0)
        back = jnp.concatenate([edge, product[PAIR:], edge], axis=0)
        main = main + forth[tap * DILATION : tap * DILATION + rows]
        mirror = mirror + back[(2 - tap) * DILATION : (2 - tap) * DILATION + rows]
    pre[0, 0:rows] = main
    pre[1, 0:rows] = mirror
    pre[:, rows:ROWS] = jnp.zeros((2, ROWS - rows, HID), F32)
    copy = pltpu.make_async_copy(pre, out, sem)
    copy.start()
    turn(normed, channels(), 1 - core(), others)
    turn(normed, channels(), core(), mine)
    copy.wait()


def slope_kernel(s0, s1, s3, s2, table, wp, taps, inner, pre, gp, bin_grad, wide, spread):
    reverse = reverser()
    pair = seat() // 2
    odd = seat() % 2
    row = lax.broadcasted_iota(jnp.int32, (128, EXONS), 0)
    owner = ((row >> 4) & 1) * 4 + ((row >> 5) ^ (seat() & 3))
    genes = jnp.where((row & 15) < 8, owner * 8 + (row & 7), -1)
    table = table()[...]
    inside = pool_inside(table, pair * PAIR - DILATION, ROWS)
    counts = dot(inside, pool_member(table, genes), 1, 1).astype(BF)
    for apart, piece in enumerate((s0, s1, s2, s3)):
        spread[apart] = piece()[...]
    wide[...] = dot(counts, spread[...].reshape(128, C), 1, 0)
    covered = wide[...].astype(BF)
    own = pl.multiple_of(odd * BINS, BINS)
    bin_grad[...] = wide[pl.ds(own, BINS + 8)][DILATION : DILATION + BINS].astype(BF)
    both = jnp.concatenate([covered, flip_channels(covered, reverse)], axis=0)
    grad_act = dot(both, wp()[...], 1, 0)

    before = jnp.maximum(2 * pair - 1, 0)
    beyond = jnp.minimum(2 * pair + 2, 7)
    left = spread[(before ^ seat()) & 3, before // 4][8 : 8 + HALO].astype(F32)
    right = spread[(beyond ^ seat()) & 3, beyond // 4][8 : 8 + HALO].astype(F32)
    halo = jnp.concatenate([jnp.where(pair > 0, left, 0.0), jnp.where(pair < 3, right, 0.0)], axis=0)
    halo = normalized(halo)
    halo = jnp.concatenate([halo, flip_channels(halo, reverse)], axis=0)
    rest = jnp.zeros((DILATION, HID), F32)
    sums = [jnp.zeros((HALO, HID), F32) for _ in range(4)]
    for tap in range(3):
        product = dot(halo, taps[tap]()[...], 1, 0)
        for branch in range(2):
            left = product[2 * HALO * branch : 2 * HALO * branch + HALO]
            right = product[2 * HALO * branch + HALO : 2 * HALO * branch + 2 * HALO]
            shift = tap if branch == 0 else 2 - tap
            if shift == 0:
                sums[2 * branch] += left
            elif shift == 1:
                sums[2 * branch] += jnp.concatenate([left[DILATION:], rest], axis=0)
                sums[2 * branch + 1] += jnp.concatenate([rest, right[:DILATION]], axis=0)
            else:
                sums[2 * branch + 1] += right
    pre[...] = inner()[...]
    for branch in range(2):
        pre[branch, 0:HALO] = pre[branch, 0:HALO] + sums[2 * branch]
        pre[branch, PAIR : PAIR + HALO] = pre[branch, PAIR : PAIR + HALO] + sums[2 * branch + 1]
    gp[0] = (grad_act[0:ROWS] * gelu_slope(pre[0])).astype(BF)
    gp[1] = (grad_act[ROWS:] * gelu_slope(pre[1])).astype(BF)


def weight_kernel(turned, turned_other, own, other, after, out, done):
    del after
    done[...] = jnp.zeros((8, 128), F32)
    wide = [[ref()[branch].astype(F32) for branch in range(2)] for ref in (own, other)]
    for tap in range(3):
        total = jnp.zeros((QUARTER, HID), F32)
        for ref, grads in zip((turned, turned_other), wide):
            main = grads[0][(2 - tap) * DILATION : (2 - tap) * DILATION + PAIR]
            mirror = grads[1][tap * DILATION : tap * DILATION + PAIR]
            total = total + dot(ref()[...], jnp.concatenate([main, mirror], axis=0).astype(BF), 1, 0)
        out[:, tap] = (total * (1.0 / 32)).astype(BF).reshape(8, 48, HID)


def plane_sum_kernel(terms, after, out):
    del after
    total = terms[0].astype(F32)
    for k in range(1, 8):
        total = total + terms[k].astype(F32)
    for k in range(8):
        out[k] = total[:, 6 * k : 6 * k + 6].astype(BF)


def column_sum_kernel(terms, out):
    total = terms[0].astype(F32)
    for k in range(1, 8):
        total = total + terms[k].astype(F32)
    for tap in range(3):
        out[:, tap] = total[tap]


def output_kernel(tok, partner, pre, wp, table, give, keep, done):
    done[...] = jnp.zeros((8, 128), F32)
    odd = seat() % 2
    pre = pre()
    acts = [gelu_value(pre[branch][DILATION : DILATION + PAIR]).astype(BF) for branch in range(2)]
    outs = dot(jnp.concatenate(acts, axis=0), wp()[...], 1, 1).astype(BF)
    mirror = flip_channels(outs[PAIR:], reverser())
    low, high = in_order(odd, tok()[...].astype(F32), partner()[...].astype(F32))
    block = jnp.concatenate([low, high], axis=0)
    block = (block + outs[0:PAIR].astype(F32) + mirror.astype(F32)).astype(BF)
    table = table()[...]
    inside = pool_inside(table, (seat() // 2) * PAIR, PAIR)
    row = lax.broadcasted_iota(jnp.int32, (GENES // 2, table.shape[1]), 0)
    genes = (row >> 3) * 16 + odd * 8 + (row & 7)
    counts = dot(pool_member(table, genes), inside, 1, 1).astype(BF)
    partial = dot(counts, block, 1, 0)
    half = (seat() // 2) % 2
    low = jnp.concatenate([partial[0:8], partial[16:24]], axis=0)
    high = jnp.concatenate([partial[8:16], partial[24:32]], axis=0)
    give[...] = jnp.where(half == 0, high, low).astype(BF)
    keep[...] = jnp.where(half == 0, low, high)


def input_kernel(tok, gp, bin_grad, taps, after, out, done):
    del after
    done[...] = jnp.zeros((8, 128), F32)
    odd = seat() % 2
    wide = tok()[...].astype(F32)
    scale = row_scale(wide)
    unit = wide * scale
    reverse = reverser()
    mirror_unit = flip_channels(tok()[...], reverse).astype(F32) * scale
    start = pl.multiple_of(odd * BINS, BINS)
    shifted = [gp()[branch, pl.ds(start, BINS + 16)].astype(F32) for branch in range(2)]
    total = jnp.zeros((2 * BINS, C), F32)
    for tap in range(3):
        main = shifted[0][(2 - tap) * DILATION : (2 - tap) * DILATION + BINS]
        mirror = shifted[1][tap * DILATION : tap * DILATION + BINS]
        total = total + dot(jnp.concatenate([main, mirror], axis=0).astype(BF), taps[tap]()[...], 1, 1)
    parts = []
    for grad, part in ((total[0:BINS], unit), (total[BINS:], mirror_unit)):
        centred = grad - part * jnp.mean(grad * part, axis=1, keepdims=True)
        parts.append((centred * scale).astype(BF))
    mirror = flip_channels(parts[1], reverse)
    out[...] = (bin_grad()[...].astype(F32) + parts[0].astype(F32) + mirror.astype(F32)).astype(BF)


def shape(dims, kind):
    return jax.ShapeDtypeStruct(dims, kind)


class Fetched:
    def __init__(self, source, buffer, sem):
        self.copy = pltpu.make_async_copy(source, buffer, sem)
        self.buffer = buffer
        self.waits = True
        self.copy.start()

    def __call__(self):
        if self.waits:
            self.copy.wait()
            self.waits = False
        return self.buffer


def call(kernel, out_shape, *args, order=(), large=(), far=(), pinned=False, scratch=(), work=1):
    outs = len(out_shape) if isinstance(out_shape, tuple) else 1
    places = [pl.BlockSpec(memory_space=pltpu.HBM if at in far else None) for at in range(outs)]
    count = len(args)
    if pinned:
        specs = [pl.BlockSpec(memory_space=pltpu.VMEM)] * count
        body, buffers = kernel, []
    else:
        args = list(args)
        specs = [pl.BlockSpec(memory_space=pl.ANY)] * count
        for at in large:
            specs[at] = pl.BlockSpec(memory_space=pltpu.HBM)
            args[at] = pltpu.with_memory_space_constraint(args[at], pltpu.HBM)
        fetched = [at for at in range(count) if at not in order]
        tapped = [at for at in fetched if args[at].shape == (3, C, HID)]
        buffers = [pltpu.VMEM(args[at].shape, args[at].dtype) for at in fetched]
        buffers.append(pltpu.SemaphoreType.DMA((len(fetched) + 2,)))

        def body(*refs):
            values = list(refs[:count])
            held = refs[count + outs : count + outs + len(fetched)]
            sems = refs[count + outs + len(fetched)]
            for k, at in enumerate(fetched):
                if at in tapped:
                    lanes = [k, len(fetched), len(fetched) + 1]
                    values[at] = [
                        Fetched(refs[at].at[tap], held[k].at[tap], sems.at[lanes[tap]])
                        for tap in range(3)
                    ]
                else:
                    values[at] = Fetched(refs[at], held[k], sems.at[k])
            kernel(*values, *refs[count : count + outs], *refs[count + outs + len(fetched) + 1 :])

    return pl.pallas_call(
        body,
        out_shape=out_shape,
        in_specs=specs,
        out_specs=tuple(places) if isinstance(out_shape, tuple) else places[0],
        scratch_shapes=buffers + list(scratch),
        cost_estimate=pl.CostEstimate(flops=int(work * 1e9), transcendentals=0, bytes_accessed=0),
        compiler_params=pltpu.CompilerParams(vmem_limit_bytes=VMEM_LIMIT),
    )(*args)


def pack(tok, grads):
    return pl.pallas_call(
        pack_kernel,
        grid=(1,),
        out_shape=shape((16, C), BF),
        in_specs=[
            pl.BlockSpec((HALO, C), lambda i: (0, 0)),
            pl.BlockSpec((HALO, C), lambda i: (BINS // HALO - 1, 0)),
            pl.BlockSpec((8, C), lambda i: (0, 0)),
        ],
        out_specs=pl.BlockSpec((16, C), lambda i: (0, 0)),
    )(tok, tok, grads)


DONE = jax.ShapeDtypeStruct((8, 128), F32)


def scatter_genes(give, keep):
    values = keep + lax.ppermute(give, "seq", [(s, s ^ 2) for s in range(8)]).astype(F32)
    upper = seat() // 4
    keep = jnp.where(upper == 0, values[:8], values[8:])
    give = jnp.where(upper == 0, values[8:], values[:8]).astype(BF)
    return keep + lax.ppermute(give, "seq", [(s, s ^ 4) for s in range(8)]).astype(F32)


def local(tokens, w_conv, w_point, exon_table, gene_grads):
    tok = tokens[0]
    table = exon_table[0]
    taps = jnp.transpose(w_conv, (1, 0, 2))
    pair_rows = shape((2, ROWS, HID), F32)

    partner = lax.ppermute(tok, "seq", SEQ_PAIRS)
    mine = pack(tok, gene_grads[0])
    across = lax.ppermute(mine, "seq", [(s, s ^ 4) for s in range(8)])
    both, ready = call(
        both_kernel, (shape((2, 16, C), BF), DONE), mine, across, work=SUM_WORK
    )
    spread = [both]
    for apart in (1, 3, 2):
        spread.append(lax.ppermute(both, "seq", [(s, s ^ apart) for s in range(8)]))

    quarter = shape((QUARTER, 2 * PAIR), BF)
    inner, turned, lent = call(
        forward_kernel,
        (pair_rows, quarter, quarter),
        tok,
        partner,
        taps,
        jnp.asarray(CHANNELS),
        ready,
        large=(0, 2),
        order=(4,),
        far=(0,),
        scratch=[pltpu.VMEM((2, ROWS, HID), F32), pltpu.SemaphoreType.DMA],
        work=FORWARD_WORK,
    )
    turned_other = lax.ppermute(lent, "batch", CORE_PAIRS)
    pre, gp, bin_grad = call(
        slope_kernel,
        (pair_rows, shape((2, ROWS, HID), BF), shape((BINS, C), BF)),
        *spread,
        table,
        w_point,
        taps,
        inner,
        large=(5, 6),
        work=SLOPE_WORK,
        scratch=[pltpu.VMEM((ROWS, C), F32), pltpu.VMEM((4, 2, 16, C), BF)],
    )
    gp_other = lax.ppermute(gp, "batch", CORE_PAIRS)
    give, keep, output_done = call(
        output_kernel,
        (shape((GENES // 4, C), BF), shape((GENES // 4, C), F32), DONE),
        tok,
        partner,
        pre,
        w_point,
        table,
        large=(0, 3),
        work=OUTPUT_WORK,
    )
    pooled = scatter_genes(give, keep)
    terms, terms_done = call(
        weight_kernel,
        (shape((8, 3, 48, HID), BF), DONE),
        turned,
        turned_other,
        gp,
        gp_other,
        output_done,
        order=(4,),
    )
    grad_input, input_done = call(
        input_kernel,
        (shape((BINS, C), BF), DONE),
        tok,
        gp,
        bin_grad,
        taps,
        terms_done,
        large=(0, 3),
        order=(4,),
        work=INPUT_WORK,
    )
    terms = lax.all_to_all(terms, ("batch", "seq"), 0, 0, tiled=True, axis_index_groups=PLANES)
    terms = call(
        plane_sum_kernel, shape((8, 3, 6, HID), BF), terms, input_done, pinned=True, work=SUM_WORK
    )
    terms = lax.all_to_all(terms, ("batch", "seq"), 0, 0, tiled=True, axis_index_groups=COLUMNS)
    total = call(column_sum_kernel, shape((6, 3, HID), F32), terms, pinned=True, work=SUM_WORK)
    return (pooled[None], grad_input[None], total)


def solution(mesh):
    placed = (P("batch", "seq", None), P(), P(), P("batch", None, None), P("batch", "seq", None))
    return jax.shard_map(
        local,
        mesh=mesh,
        in_specs=placed,
        out_specs=(
            P("batch", "seq", None),
            P("batch", "seq", None),
            P(("batch", "seq"), None, None),
        ),
        check_vma=False,
    )
```

```python
import jax
import jax.numpy as jnp
import numpy as np
from jax import lax
from jax.experimental import pallas as pl
from jax.experimental.pallas import tpu as pltpu
from jax.sharding import PartitionSpec as P

DILATION = 4
GENES = 64
EXONS = 256
EPSILON = 1e-06
INVERSE_ROOT_TWO = 0.7071067811865476
INVERSE_ROOT_TAU = 0.3989422804014327

BINS = 128
PAIR = 2 * BINS
HALO = 8
ROWS = PAIR + 2 * HALO
C = 1536
HID = 384
QUARTER = C // 4
FLIP = 256
BF = jnp.bfloat16
F32 = jnp.float32
VMEM_LIMIT = 28 * 1024 * 1024

FORWARD_WORK = 0.5
SLOPE_WORK = 2
OUTPUT_WORK = 0.3
INPUT_WORK = 0.9
SUM_WORK = 1
CORE_PAIRS = [(b, b ^ 1) for b in range(32)]
SEQ_PAIRS = [(s, s ^ 1) for s in range(8)]


def linear(z_hi, x, z_lo, y, core):
    return ((z_lo * 4 + y) * 2 + core) * 8 + z_hi * 4 + x


PLANES = [
    [linear(zh, 2 * half + odd, zl, y, c) for y in range(4) for half in range(2)]
    for odd in range(2)
    for zh in range(2)
    for zl in range(4)
    for c in range(2)
]
COLUMNS = [
    [linear(zh, x, zl, y, c) for zh in range(2) for zl in range(4)]
    for x in range(4)
    for y in range(4)
    for c in range(2)
]
CHANNELS = np.array(
    [
        6 * linear(zh, 2 * half, zl, y, 0) + k
        for y in range(4)
        for half in range(2)
        for zh in range(2)
        for zl in range(4)
        for k in range(6)
    ],
    dtype=np.int32,
).reshape(QUARTER, 1)


def dot(a, b, da, db):
    return lax.dot_general(a, b, (((da,), (db,)), ((), ())), preferred_element_type=F32)


def cumulative(values):
    return 0.5 * (1.0 + lax.erf(values * INVERSE_ROOT_TWO))


def gelu_value(values):
    return values * cumulative(values)


def gelu_slope(values):
    return cumulative(values) + values * jnp.exp(-0.5 * values * values) * INVERSE_ROOT_TAU


def reverser():
    rows = lax.broadcasted_iota(jnp.int32, (FLIP, FLIP), 0)
    cols = lax.broadcasted_iota(jnp.int32, (FLIP, FLIP), 1)
    return jnp.where(rows + cols == FLIP - 1, 1.0, 0.0).astype(BF)


def flip_channels(values, turn):
    parts = []
    for k in reversed(range(C // FLIP)):
        parts.append(dot(values[:, k * FLIP : (k + 1) * FLIP], turn, 1, 0).astype(BF))
    return jnp.concatenate(parts, axis=1)


def row_scale(wide):
    return lax.rsqrt(jnp.mean(wide * wide, axis=1, keepdims=True) + EPSILON)


def pool_inside(table, first_bin, rows):
    positions = first_bin + lax.broadcasted_iota(jnp.int32, (rows, table.shape[1]), 0)
    inside = (positions >= table[1:2, :]) & (positions < table[2:3, :])
    return jnp.where(inside, 1.0, 0.0).astype(BF)


def pool_member(table, genes):
    return jnp.where(genes == table[0:1, :], 1.0, 0.0).astype(BF)


def seat():
    return lax.axis_index("seq").astype(jnp.int32)


def core():
    return lax.axis_index("batch").astype(jnp.int32) % 2


def pack_kernel(head, tail, grads, out):
    edge = jnp.where(seat() % 2 == 1, tail[...].astype(F32), head[...].astype(F32))
    out[...] = jnp.concatenate([grads[...].astype(F32), edge], axis=0).astype(BF)


def both_kernel(mine, across, out, done):
    upper = seat() // 4
    low, high = in_order(upper, mine()[...].astype(F32), across()[...].astype(F32))
    out[0] = low.astype(BF)
    out[1] = high.astype(BF)
    done[...] = jnp.zeros((8, 128), F32)


def in_order(odd, own, partner):
    return jnp.where(odd == 0, own, partner), jnp.where(odd == 0, partner, own)


def normalized(wide):
    return (wide * row_scale(wide)).astype(BF)


def turn(normed, channels, core_index, out):
    wanted = channels[...] + 6 * (seat() % 2) + 48 * core_index
    main = jnp.zeros((QUARTER, PAIR), F32)
    mirror = jnp.zeros((QUARTER, PAIR), F32)
    for k in range(C // FLIP):
        lane = k * FLIP + lax.broadcasted_iota(jnp.int32, (QUARTER, FLIP), 1)
        piece = normed[:, k * FLIP : (k + 1) * FLIP]
        pick = jnp.where(lane == wanted, 1.0, 0.0).astype(BF)
        main = main + dot(pick, piece, 1, 1)
        pick = jnp.where(C - 1 - lane == wanted, 1.0, 0.0).astype(BF)
        mirror = mirror + dot(pick, piece, 1, 1)
    out[:, 0:PAIR] = main.astype(BF)
    out[:, PAIR:] = mirror.astype(BF)


def forward_kernel(tok, partner, taps, channels, after, out, mine, others, pre, sem):
    del after
    low, high = in_order(seat() % 2, tok()[...].astype(F32), partner()[...].astype(F32))
    normed = normalized(jnp.concatenate([low, high], axis=0))
    turn(normed, channels(), 1 - core(), others)
    both = jnp.concatenate([normed, flip_channels(normed, reverser())], axis=0)
    rows = PAIR + 2 * DILATION
    edge = jnp.zeros((HALO, HID), F32)
    main = jnp.zeros((rows, HID), F32)
    mirror = jnp.zeros((rows, HID), F32)
    for tap in range(3):
        product = dot(both, taps[tap]()[...], 1, 0)
        forth = jnp.concatenate([edge, product[0:PAIR], edge], axis=0)
        back = jnp.concatenate([edge, product[PAIR:], edge], axis=0)
        main = main + forth[tap * DILATION : tap * DILATION + rows]
        mirror = mirror + back[(2 - tap) * DILATION : (2 - tap) * DILATION + rows]
    pre[0, 0:rows] = main
    pre[1, 0:rows] = mirror
    pre[:, rows:ROWS] = jnp.zeros((2, ROWS - rows, HID), F32)
    copy = pltpu.make_async_copy(pre, out, sem)
    copy.start()
    turn(normed, channels(), core(), mine)
    copy.wait()


def slope_kernel(s0, s1, s3, s2, table, wp, taps, inner, pre, gp, bin_grad, wide, spread):
    reverse = reverser()
    pair = seat() // 2
    odd = seat() % 2
    row = lax.broadcasted_iota(jnp.int32, (128, EXONS), 0)
    owner = ((row >> 4) & 1) * 4 + ((row >> 5) ^ (seat() & 3))
    genes = jnp.where((row & 15) < 8, owner * 8 + (row & 7), -1)
    table = table()[...]
    inside = pool_inside(table, pair * PAIR - DILATION, ROWS)
    counts = dot(inside, pool_member(table, genes), 1, 1).astype(BF)
    for apart, piece in enumerate((s0, s1, s2, s3)):
        spread[apart] = piece()[...]
    wide[...] = dot(counts, spread[...].reshape(128, C), 1, 0)
    covered = wide[...].astype(BF)
    own = pl.multiple_of(odd * BINS, BINS)
    bin_grad[...] = wide[pl.ds(own, BINS + 8)][DILATION : DILATION + BINS].astype(BF)
    both = jnp.concatenate([covered, flip_channels(covered, reverse)], axis=0)
    grad_act = dot(both, wp()[...], 1, 0)

    before = jnp.maximum(2 * pair - 1, 0)
    beyond = jnp.minimum(2 * pair + 2, 7)
    left = spread[(before ^ seat()) & 3, before // 4][8 : 8 + HALO].astype(F32)
    right = spread[(beyond ^ seat()) & 3, beyond // 4][8 : 8 + HALO].astype(F32)
    halo = jnp.concatenate([jnp.where(pair > 0, left, 0.0), jnp.where(pair < 3, right, 0.0)], axis=0)
    halo = normalized(halo)
    halo = jnp.concatenate([halo, flip_channels(halo, reverse)], axis=0)
    rest = jnp.zeros((DILATION, HID), F32)
    sums = [jnp.zeros((HALO, HID), F32) for _ in range(4)]
    for tap in range(3):
        product = dot(halo, taps[tap]()[...], 1, 0)
        for branch in range(2):
            left = product[2 * HALO * branch : 2 * HALO * branch + HALO]
            right = product[2 * HALO * branch + HALO : 2 * HALO * branch + 2 * HALO]
            shift = tap if branch == 0 else 2 - tap
            if shift == 0:
                sums[2 * branch] += left
            elif shift == 1:
                sums[2 * branch] += jnp.concatenate([left[DILATION:], rest], axis=0)
                sums[2 * branch + 1] += jnp.concatenate([rest, right[:DILATION]], axis=0)
            else:
                sums[2 * branch + 1] += right
    pre[...] = inner()[...]
    for branch in range(2):
        pre[branch, 0:HALO] = pre[branch, 0:HALO] + sums[2 * branch]
        pre[branch, PAIR : PAIR + HALO] = pre[branch, PAIR : PAIR + HALO] + sums[2 * branch + 1]
    gp[0] = (grad_act[0:ROWS] * gelu_slope(pre[0])).astype(BF)
    gp[1] = (grad_act[ROWS:] * gelu_slope(pre[1])).astype(BF)


def weight_kernel(turned, turned_other, own, other, after, out, done):
    del after
    done[...] = jnp.zeros((8, 128), F32)
    wide = [[ref()[branch].astype(F32) for branch in range(2)] for ref in (own, other)]
    for tap in range(3):
        total = jnp.zeros((QUARTER, HID), F32)
        for ref, grads in zip((turned, turned_other), wide):
            main = grads[0][(2 - tap) * DILATION : (2 - tap) * DILATION + PAIR]
            mirror = grads[1][tap * DILATION : tap * DILATION + PAIR]
            total = total + dot(ref()[...], jnp.concatenate([main, mirror], axis=0).astype(BF), 1, 0)
        out[:, tap] = (total * (1.0 / 32)).astype(BF).reshape(8, 48, HID)


def plane_sum_kernel(terms, after, out):
    del after
    total = terms[0].astype(F32)
    for k in range(1, 8):
        total = total + terms[k].astype(F32)
    for k in range(8):
        out[k] = total[:, 6 * k : 6 * k + 6].astype(BF)


def column_sum_kernel(terms, out):
    total = terms[0].astype(F32)
    for k in range(1, 8):
        total = total + terms[k].astype(F32)
    for tap in range(3):
        out[:, tap] = total[tap]


def output_kernel(tok, partner, pre, wp, table, give, keep, done):
    done[...] = jnp.zeros((8, 128), F32)
    odd = seat() % 2
    pre = pre()
    acts = [gelu_value(pre[branch][DILATION : DILATION + PAIR]).astype(BF) for branch in range(2)]
    outs = dot(jnp.concatenate(acts, axis=0), wp()[...], 1, 1).astype(BF)
    mirror = flip_channels(outs[PAIR:], reverser())
    low, high = in_order(odd, tok()[...].astype(F32), partner()[...].astype(F32))
    block = jnp.concatenate([low, high], axis=0)
    block = (block + outs[0:PAIR].astype(F32) + mirror.astype(F32)).astype(BF)
    table = table()[...]
    inside = pool_inside(table, (seat() // 2) * PAIR, PAIR)
    row = lax.broadcasted_iota(jnp.int32, (GENES // 2, table.shape[1]), 0)
    genes = (row >> 3) * 16 + odd * 8 + (row & 7)
    counts = dot(pool_member(table, genes), inside, 1, 1).astype(BF)
    partial = dot(counts, block, 1, 0)
    half = (seat() // 2) % 2
    low = jnp.concatenate([partial[0:8], partial[16:24]], axis=0)
    high = jnp.concatenate([partial[8:16], partial[24:32]], axis=0)
    give[...] = jnp.where(half == 0, high, low).astype(BF)
    keep[...] = jnp.where(half == 0, low, high)


def input_kernel(tok, gp, bin_grad, taps, after, out, done):
    del after
    done[...] = jnp.zeros((8, 128), F32)
    odd = seat() % 2
    wide = tok()[...].astype(F32)
    scale = row_scale(wide)
    unit = wide * scale
    reverse = reverser()
    mirror_unit = flip_channels(tok()[...], reverse).astype(F32) * scale
    start = pl.multiple_of(odd * BINS, BINS)
    shifted = [gp()[branch, pl.ds(start, BINS + 16)].astype(F32) for branch in range(2)]
    total = jnp.zeros((2 * BINS, C), F32)
    for tap in range(3):
        main = shifted[0][(2 - tap) * DILATION : (2 - tap) * DILATION + BINS]
        mirror = shifted[1][tap * DILATION : tap * DILATION + BINS]
        total = total + dot(jnp.concatenate([main, mirror], axis=0).astype(BF), taps[tap]()[...], 1, 1)
    parts = []
    for grad, part in ((total[0:BINS], unit), (total[BINS:], mirror_unit)):
        centred = grad - part * jnp.mean(grad * part, axis=1, keepdims=True)
        parts.append((centred * scale).astype(BF))
    mirror = flip_channels(parts[1], reverse)
    out[...] = (bin_grad()[...].astype(F32) + parts[0].astype(F32) + mirror.astype(F32)).astype(BF)


def shape(dims, kind):
    return jax.ShapeDtypeStruct(dims, kind)


class Fetched:
    def __init__(self, source, buffer, sem):
        self.copy = pltpu.make_async_copy(source, buffer, sem)
        self.buffer = buffer
        self.waits = True
        self.copy.start()

    def __call__(self):
        if self.waits:
            self.copy.wait()
            self.waits = False
        return self.buffer


def call(kernel, out_shape, *args, order=(), large=(), far=(), pinned=False, scratch=(), work=1):
    outs = len(out_shape) if isinstance(out_shape, tuple) else 1
    places = [pl.BlockSpec(memory_space=pltpu.HBM if at in far else None) for at in range(outs)]
    count = len(args)
    if pinned:
        specs = [pl.BlockSpec(memory_space=pltpu.VMEM)] * count
        body, buffers = kernel, []
    else:
        args = list(args)
        specs = [pl.BlockSpec(memory_space=pl.ANY)] * count
        for at in large:
            specs[at] = pl.BlockSpec(memory_space=pltpu.HBM)
            args[at] = pltpu.with_memory_space_constraint(args[at], pltpu.HBM)
        fetched = [at for at in range(count) if at not in order]
        tapped = [at for at in fetched if args[at].shape == (3, C, HID)]
        buffers = [pltpu.VMEM(args[at].shape, args[at].dtype) for at in fetched]
        buffers.append(pltpu.SemaphoreType.DMA((len(fetched) + 2,)))

        def body(*refs):
            values = list(refs[:count])
            held = refs[count + outs : count + outs + len(fetched)]
            sems = refs[count + outs + len(fetched)]
            for k, at in enumerate(fetched):
                if at in tapped:
                    lanes = [k, len(fetched), len(fetched) + 1]
                    values[at] = [
                        Fetched(refs[at].at[tap], held[k].at[tap], sems.at[lanes[tap]])
                        for tap in range(3)
                    ]
                else:
                    values[at] = Fetched(refs[at], held[k], sems.at[k])
            kernel(*values, *refs[count : count + outs], *refs[count + outs + len(fetched) + 1 :])

    return pl.pallas_call(
        body,
        out_shape=out_shape,
        in_specs=specs,
        out_specs=tuple(places) if isinstance(out_shape, tuple) else places[0],
        scratch_shapes=buffers + list(scratch),
        cost_estimate=pl.CostEstimate(flops=int(work * 1e9), transcendentals=0, bytes_accessed=0),
        compiler_params=pltpu.CompilerParams(vmem_limit_bytes=VMEM_LIMIT),
    )(*args)


def pack(tok, grads):
    return pl.pallas_call(
        pack_kernel,
        grid=(1,),
        out_shape=shape((16, C), BF),
        in_specs=[
            pl.BlockSpec((HALO, C), lambda i: (0, 0)),
            pl.BlockSpec((HALO, C), lambda i: (BINS // HALO - 1, 0)),
            pl.BlockSpec((8, C), lambda i: (0, 0)),
        ],
        out_specs=pl.BlockSpec((16, C), lambda i: (0, 0)),
    )(tok, tok, grads)


DONE = jax.ShapeDtypeStruct((8, 128), F32)


def scatter_genes(give, keep):
    values = keep + lax.ppermute(give, "seq", [(s, s ^ 2) for s in range(8)]).astype(F32)
    upper = seat() // 4
    keep = jnp.where(upper == 0, values[:8], values[8:])
    give = jnp.where(upper == 0, values[8:], values[:8]).astype(BF)
    return keep + lax.ppermute(give, "seq", [(s, s ^ 4) for s in range(8)]).astype(F32)


def local(tokens, w_conv, w_point, exon_table, gene_grads):
    tok = tokens[0]
    table = exon_table[0]
    taps = jnp.transpose(w_conv, (1, 0, 2))
    pair_rows = shape((2, ROWS, HID), F32)

    partner = lax.ppermute(tok, "seq", SEQ_PAIRS)
    mine = pack(tok, gene_grads[0])
    across = lax.ppermute(mine, "seq", [(s, s ^ 4) for s in range(8)])
    both, ready = call(
        both_kernel, (shape((2, 16, C), BF), DONE), mine, across, work=SUM_WORK
    )
    spread = [both]
    for apart in (1, 3, 2):
        spread.append(lax.ppermute(both, "seq", [(s, s ^ apart) for s in range(8)]))

    quarter = shape((QUARTER, 2 * PAIR), BF)
    inner, turned, lent = call(
        forward_kernel,
        (pair_rows, quarter, quarter),
        tok,
        partner,
        taps,
        jnp.asarray(CHANNELS),
        ready,
        large=(0, 2),
        order=(4,),
        far=(0,),
        scratch=[pltpu.VMEM((2, ROWS, HID), F32), pltpu.SemaphoreType.DMA],
        work=FORWARD_WORK,
    )
    turned_other = lax.ppermute(lent, "batch", CORE_PAIRS)
    pre, gp, bin_grad = call(
        slope_kernel,
        (pair_rows, shape((2, ROWS, HID), BF), shape((BINS, C), BF)),
        *spread,
        table,
        w_point,
        taps,
        inner,
        large=(5, 6),
        work=SLOPE_WORK,
        scratch=[pltpu.VMEM((ROWS, C), F32), pltpu.VMEM((4, 2, 16, C), BF)],
    )
    gp_other = lax.ppermute(gp, "batch", CORE_PAIRS)
    give, keep, output_done = call(
        output_kernel,
        (shape((GENES // 4, C), BF), shape((GENES // 4, C), F32), DONE),
        tok,
        partner,
        pre,
        w_point,
        table,
        large=(0, 3),
        work=OUTPUT_WORK,
    )
    pooled = scatter_genes(give, keep)
    terms, terms_done = call(
        weight_kernel,
        (shape((8, 3, 48, HID), BF), DONE),
        turned,
        turned_other,
        gp,
        gp_other,
        output_done,
        order=(4,),
    )
    grad_input, input_done = call(
        input_kernel,
        (shape((BINS, C), BF), DONE),
        tok,
        gp,
        bin_grad,
        taps,
        terms_done,
        large=(0, 3),
        order=(4,),
        work=INPUT_WORK,
    )
    terms = lax.all_to_all(terms, ("batch", "seq"), 0, 0, tiled=True, axis_index_groups=PLANES)
    terms = call(
        plane_sum_kernel, shape((8, 3, 6, HID), BF), terms, input_done, pinned=True, work=SUM_WORK
    )
    terms = lax.all_to_all(terms, ("batch", "seq"), 0, 0, tiled=True, axis_index_groups=COLUMNS)
    total = call(column_sum_kernel, shape((6, 3, HID), F32), terms, pinned=True, work=SUM_WORK)
    return (pooled[None], grad_input[None], total)


def solution(mesh):
    placed = (P("batch", "seq", None), P(), P(), P("batch", None, None), P("batch", "seq", None))
    return jax.shard_map(
        local,
        mesh=mesh,
        in_specs=placed,
        out_specs=(
            P("batch", "seq", None),
            P("batch", "seq", None),
            P(("batch", "seq"), None, None),
        ),
        check_vma=False,
    )
```
